128 devices in a mesh: site: 4 (over z), blk: 16 (over x, y), charge: 2 (over core).
Axes of the slice: x: 4, y: 4, z: 4, core: 2. Of those that a mesh axis runs over, the one named last changes fastest.
Arguments:
- theta: bfloat16 [4, 64, 128, 2048], P('site', ('blk', 'charge')), may hold values from -6 to 6
- boundary_env: bfloat16 [64, 18, 128, 128], P(('blk', 'charge')), may hold values from -1 to 1
- right_env: bfloat16 [4, 64, 18, 128, 128], P('site', ('blk', 'charge')), may hold values from -1 to 1
- site_tensors: bfloat16 [4, 2, 64, 4, 128, 128], P('site', None, ('blk', 'charge')), may hold values from -0.375 to 0.375
- site_mpo: bfloat16 [4, 2, 18, 18, 4, 4], P('site'), may hold values from -0.75 to 0.75
- bond_ops: bfloat16 [4, 18, 16, 16], P('site'), may hold values from -1 to 1
- block_energy: float32 [4, 64], P('site', ('blk', 'charge')), may hold values from 1 to 4
- sector_charge: int32 [4, 64], P('site', ('blk', 'charge')), may hold values from 0 to 63, as said below
- block_len: int32 [4, 64], P('site', ('blk', 'charge')), may hold values from 64 to 128
- channel_charge: int32 [18], replicated, may hold values from -1 to 1
Outputs:
- env_out: bfloat16 [4, 64, 18, 128, 128], P('site', ('blk', 'charge'))
- lanczos: bfloat16 [4, 64, 128, 2048], P('site', ('blk', 'charge'))
- coefficients: float32 [4, 2], P('site')
The draws below stay inside these ranges and needn't reach their ends.
Inputs may be any that keep to these rules, and one draw needn't show every extreme that they name: `sector_charge`: in each section every label of 0 to 63 appears exactly once; the blocks held at index c of the charge axis carry labels of parity c.
All inputs are finite; a program needn't handle non-finite values.
Results may differ from the reference program's by a relative error of at most 0.03.
Values may be sent and summed in bfloat16 or wider, within the bound.
A program may use at most 128 MiB of HBM per device.

```python
import math
import jax
import jax.numpy as jnp
from jax import lax

BS = 128
PH = 4
WCH = 18
PP = 16
M = 2048
NS = 64
SEC_DEV = 2
SECTIONS = 4


def draw_sector_charge(key, part):
    half_count = NS // 2

    def one_section(subkey):
        first_key, second_key = jax.random.split(subkey)
        evens = 2 * jax.random.permutation(first_key, half_count)
        odds = 2 * jax.random.permutation(second_key, half_count) + 1
        joined = jnp.stack([evens.reshape(-1, SEC_DEV), odds.reshape(-1, SEC_DEV)], axis=1)
        return joined.reshape(NS).astype(jnp.int32)
    return jax.vmap(one_section)(jax.random.split(key, SECTIONS))


def drawn_noise(key, shape, spread):
    values = jax.random.truncated_normal(key, -6.0, 6.0, shape, jnp.float32) * spread
    return jnp.clip(values, -1.0, 1.0)


def draw_boundary_env(key, part):
    own_key = jax.random.fold_in(key, 101)
    shape = (NS, WCH, BS, BS)
    spread = float(BS) ** (-0.5)
    values = drawn_noise(own_key, shape, spread)
    return values.astype(jnp.bfloat16)


def draw_right_env(key, part):
    own_key = jax.random.fold_in(key, 202)
    shape = (SECTIONS, NS, WCH, BS, BS)
    spread = float(BS) ** (-0.5)
    values = drawn_noise(own_key, shape, spread)
    return values.astype(jnp.bfloat16)


def draw_bond_ops(key, part):
    own_key = jax.random.fold_in(key, 303)
    shape = (SECTIONS, WCH, PP, PP)
    spread = float(PP * 4) ** (-0.5)
    values = drawn_noise(own_key, shape, spread)
    return values.astype(jnp.bfloat16)


def set_ends(values, key, low, largest):
    shape = values.shape
    index_at = [jax.random.randint(jax.random.fold_in(key, axis), (), 0, shape[axis]) for axis in range(len(shape))]
    values = values.at[tuple(index_at)].set(low)
    longest = shape.index(max(shape))
    index_at[longest] = (index_at[longest] + 1) % shape[longest]
    return values.at[tuple(index_at)].set(largest)


def block_scale(stream_key, shape, cuts, least, top_value):
    gain, own = 1.0, jax.random.fold_in(stream_key, 6)
    for dim, blocks in cuts:
        heights = jnp.exp(jax.random.uniform(jax.random.fold_in(own, dim), (blocks,), jnp.float32, least / len(cuts), top_value / len(cuts)))
        gain = gain * jnp.repeat(heights, shape[dim] // blocks).reshape([-1 if axis == dim else 1 for axis in range(len(shape))])
    return gain


def normal_values(key, dims, scale, bound, cuts=(), held_as=jnp.bfloat16):
    values = scale * jax.random.normal(key, dims, jnp.float32)
    if cuts:
        values = values * block_scale(key, dims, cuts, -0.22, 0.18)
    return jnp.clip(values, -bound, bound).astype(held_as)


def setup_inputs(seed: int = 0) -> dict:
    arg_keys = jax.random.split(jax.random.key(seed), 11)
    theta = normal_values(arg_keys[0], (SECTIONS, NS, BS, M), 1.0, 6.0, ((0, 4), (1, 32)))
    boundary_env = draw_boundary_env(jax.random.fold_in(arg_keys[10], 71), 0)
    right_env = draw_right_env(jax.random.fold_in(arg_keys[10], 71), 0)
    site_tensors = normal_values(arg_keys[3], (SECTIONS, 2, NS, PH, BS, BS), (BS * PH // 2) ** -0.5, 0.375, ((0, 4), (2, 32)))
    site_mpo = normal_values(arg_keys[4], (SECTIONS, 2, WCH, WCH, PH, PH), (WCH * PH) ** -0.5, 0.75, ((0, 4),))
    bond_ops = draw_bond_ops(jax.random.fold_in(arg_keys[10], 71), 0)
    block_energy = jnp.clip(jnp.exp(math.log(4.0) - 1.3862944 * jax.random.uniform(arg_keys[6], (SECTIONS, NS), jnp.float32) ** block_scale(arg_keys[6], (SECTIONS, NS), ((0, 4), (1, 32)), -0.2, 0.2)), 1.0, 4.0)
    sector_charge = draw_sector_charge(jax.random.fold_in(arg_keys[10], 71), 0)
    block_len = set_ends(jax.random.randint(arg_keys[8], (SECTIONS, NS), BS // 2, BS + 1), jax.random.fold_in(arg_keys[8], 1), BS // 2, BS).astype(jnp.int32)
    channel_charge = set_ends(jax.random.randint(arg_keys[9], (WCH,), -1, 2), jax.random.fold_in(arg_keys[9], 1), -1, 1).astype(jnp.int32)
    return {"theta": theta, "boundary_env": boundary_env, "right_env": right_env, "site_tensors": site_tensors, "site_mpo": site_mpo, "bond_ops": bond_ops, "block_energy": block_energy, "sector_charge": sector_charge, "block_len": block_len, "channel_charge": channel_charge}


def env_update(environ, tensors, site_op):

    def one_block(entries):
        env_block, site_blocks = entries
        left_part = jnp.einsum('wab,sbc->wsac', env_block.astype(jnp.float32), site_blocks.astype(jnp.float32)).astype(jnp.bfloat16)
        mixed = jnp.einsum('wvts,wsac->vtac', site_op.astype(jnp.float32), left_part.astype(jnp.float32)).astype(jnp.bfloat16)
        return jnp.einsum('tab,vtac->vbc', site_blocks.astype(jnp.float32), mixed.astype(jnp.float32)).astype(jnp.bfloat16)
    return lax.map(one_block, (environ, tensors))

def block_product(env_block, right_blocks, chosen, ops, charges):

    def segment(total_sum, entries):
        left_block, right_block, bond_op, charge = entries
        source_tile = lax.dynamic_index_in_dim(chosen, charge + 1, 0, keepdims=False)
        contracted = jnp.dot(left_block, source_tile, preferred_element_type=jnp.float32).astype(jnp.bfloat16)
        shaped = contracted.reshape(contracted.shape[0], ops.shape[1], -1)
        applied = jnp.einsum('asb,bc->asc', shaped.astype(jnp.float32), right_block.astype(jnp.float32)).astype(jnp.bfloat16)
        final = jnp.einsum('asc,st->atc', applied.astype(jnp.float32), bond_op.astype(jnp.float32))
        return (total_sum + final.reshape(total_sum.shape), None)
    start_sum = jnp.zeros((chosen.shape[1], chosen.shape[2]), jnp.float32)
    return lax.scan(segment, start_sum, (env_block, right_blocks, ops, charges))[0]

def reference(theta, boundary_env, right_env, site_tensors, site_mpo, bond_ops, block_energy, sector_charge, block_len, channel_charge):
    environ = boundary_env
    env_list, vec_list, coef_list = ([], [], [])
    indices = jnp.arange(NS, dtype=jnp.int32)
    for section in range(SECTIONS):
        env_in = environ
        updated = env_update(env_in, site_tensors[section, 0], site_mpo[section, 0])
        updated = env_update(updated, site_tensors[section, 1], site_mpo[section, 1])
        env_list.append(updated)
        environ = updated
        labels = sector_charge[section]
        row_mask = (jnp.arange(BS, dtype=jnp.int32)[None, :] < block_len[section][:, None]).astype(jnp.float32)
        theta_m = (theta[section].astype(jnp.float32) * row_mask[:, :, None]).astype(jnp.bfloat16)
        position = jnp.zeros((NS,), jnp.int32).at[labels].set(indices)
        picked = []
        for sign in (-1, 1):
            target = labels + sign
            valid = ((target >= 0) & (target < NS)).astype(jnp.bfloat16)
            source = position[jnp.clip(target, 0, NS - 1)]
            picked.append(theta_m[source] * valid[:, None, None])
        chosen_all = jnp.stack([picked[0], theta_m, picked[1]], axis=1)
        ops = bond_ops[section]

        def per_block(entries):
            return block_product(entries[0], entries[1], entries[2], ops, channel_charge)
        product = lax.map(per_block, (env_in, right_env[section], chosen_all))
        theta_f = theta_m.astype(jnp.float32)
        product = product * row_mask[:, :, None] - block_energy[section][:, None, None] * theta_f
        rayleigh = jnp.sum(theta_f * product) / jnp.sum(theta_f * theta_f)
        residual = product - rayleigh * theta_f
        mean_sq = jnp.sum(residual * residual) / (NS * BS * M)
        vec_list.append((residual / jnp.sqrt(mean_sq + 1e-06)).astype(jnp.bfloat16))
        coef_list.append(jnp.stack([rayleigh, jnp.sqrt(mean_sq)]))
    return (jnp.stack(env_list), jnp.stack(vec_list), jnp.stack(coef_list))
```

```python
import jax
import jax.numpy as jnp
from jax import lax
from jax.experimental import pallas as pl
from jax.experimental.pallas import tpu as pltpu
from jax.sharding import PartitionSpec as P

BS = 128
PH = 4
WCH = 18
WP = 24
PP = 16
M = 2048
NS = 64
SEC = 4
NBLK = 16
NDEV = 32
F32 = jnp.float32
BF16 = jnp.bfloat16
MESH = pl.DeviceIdType.MESH
VMEM_LIMIT = 64 * 1024 * 1024 - 64 * 1024
CH = 8


def mm(a, b):
    return jnp.dot(a, b, preferred_element_type=F32)


def env_site(a_ref, w_ref, l_ref, m_ref, at_ref, out_ref):
    for t in range(PH):
        at_ref[:, t * BS : (t + 1) * BS] = a_ref[t].T
    a_cat = jnp.concatenate([a_ref[s] for s in range(PH)], axis=1)
    w2 = w_ref[:, : PH * WP]

    def chunk(ci, carry):
        base = pl.multiple_of(ci * (CH * WP), CH * WP)
        left = mm(l_ref[pl.ds(base, CH * WP), :].astype(BF16), a_cat)
        for j in range(0, CH, 2):
            sides = []
            for e in (j, j + 1):
                rows = left[e * WP : (e + 1) * WP]
                sides.append(
                    jnp.concatenate([rows[:, s * BS : (s + 1) * BS] for s in range(PH)], axis=0)
                )
            mixed = mm(w2, jnp.concatenate(sides, axis=1).astype(BF16))
            for e in range(2):
                start = pl.multiple_of((ci * CH + j + e) * (PH * WCH), 8)
                m_ref[pl.ds(start, PH * WCH), :] = mixed[: PH * WCH, e * BS : (e + 1) * BS]
        return carry

    lax.fori_loop(0, BS // CH, chunk, 0)

    def channels(vi, carry):
        sides = []
        for e in range(2):
            sides.append(
                jnp.concatenate(
                    [
                        m_ref[pl.ds(t * WCH + vi * 2 + e, BS, stride=PH * WCH), :]
                        for t in range(PH)
                    ],
                    axis=0,
                )
            )
        new = mm(at_ref[...], jnp.concatenate(sides, axis=1).astype(BF16))
        for e in range(2):
            one = new[:, e * BS : (e + 1) * BS]
            out_ref[vi * 2 + e] = one.astype(BF16)
            l_ref[pl.ds(vi * 2 + e, BS, stride=WP), :] = one
        return carry

    lax.fori_loop(0, WCH // 2, channels, 0)


def load_env(env_ref, l_ref, slot_ref):
    l_ref[...] = jnp.zeros_like(l_ref)

    def one(v, carry):
        block = env_ref[v]
        slot_ref[v] = block
        l_ref[pl.ds(v, BS, stride=WP), :] = block.astype(F32)
        return carry

    lax.fori_loop(0, WCH, one, 0)


def exchange_kernel(
    theta_ref,
    lab_ref,
    tens_ref,
    w2_ref,
    benv_ref,
    partner_ref,
    envin_ref,
    envout_ref,
    recv1,
    send2,
    lab_all,
    inv,
    lab_s,
    inv_s,
    tens,
    w2,
    left,
    mixed,
    at,
    envs,
    lab_send,
    lab_recv,
    one_send,
    one_recv,
    two_send,
    two_recv,
    ten_send,
    ten_recv,
    w_send,
    w_recv,
    local,
):
    z = lax.axis_index("site")
    blk = lax.axis_index("blk")
    core = lax.axis_index("charge")
    me = blk * 2 + core

    barrier = pltpu.get_barrier_semaphore()

    def greet(off, carry):
        dev = lax.rem(me + off, NDEV)
        pl.semaphore_signal(
            barrier,
            inc=1,
            device_id={"blk": lax.div(dev, 2), "charge": lax.rem(dev, 2)},
            device_id_type=MESH,
        )
        return carry

    lax.fori_loop(1, NDEV, greet, 0)
    for off in range(1, SEC):
        pl.semaphore_signal(
            barrier,
            inc=1,
            device_id={"site": lax.rem(z + off, SEC)},
            device_id_type=MESH,
        )
    pl.semaphore_wait(barrier, NDEV - 1 + SEC - 1)

    def labels_to(off, peer):
        dev = lax.rem(me + off, NDEV)
        return pltpu.make_async_remote_copy(
            src_ref=lab_ref,
            dst_ref=lab_all.at[me],
            send_sem=lab_send.at[off],
            recv_sem=lab_recv.at[peer],
            device_id={"blk": lax.div(dev, 2), "charge": lax.rem(dev, 2)},
            device_id_type=MESH,
        )

    def piece_to(off, peer):
        dev = lax.rem(blk + off, NBLK)
        return pltpu.make_async_remote_copy(
            src_ref=theta_ref.at[:, :, pl.ds(pl.multiple_of(dev * BS, BS), BS)],
            dst_ref=recv1.at[pl.ds(1 + 2 * blk, 2)],
            send_sem=one_send.at[off],
            recv_sem=one_recv.at[peer],
            device_id={"blk": dev},
            device_id_type=MESH,
        )

    def picked_to(off, peer):
        dev = lax.rem(blk + off, NBLK)
        return pltpu.make_async_remote_copy(
            src_ref=send2.at[dev],
            dst_ref=partner_ref.at[blk],
            send_sem=two_send.at[off],
            recv_sem=two_recv.at[peer],
            device_id={"blk": dev, "charge": 1 - core},
            device_id_type=MESH,
        )

    def tensors_to(off, sec):
        return pltpu.make_async_remote_copy(
            src_ref=tens_ref,
            dst_ref=tens.at[z],
            send_sem=ten_send.at[off],
            recv_sem=ten_recv.at[sec],
            device_id={"site": lax.rem(z + off, SEC)},
            device_id_type=MESH,
        )

    def mixer_to(off, sec):
        return pltpu.make_async_remote_copy(
            src_ref=w2_ref,
            dst_ref=w2.at[z],
            send_sem=w_send.at[off],
            recv_sem=w_recv.at[sec],
            device_id={"site": lax.rem(z + off, SEC)},
            device_id_type=MESH,
        )

    def loop(low, high, body):
        def step(i, carry):
            body(i)
            return carry

        lax.fori_loop(low, high, step, 0)

    loop(1, NDEV, lambda off: labels_to(off, me).start())
    loop(1, NBLK, lambda off: piece_to(off, blk).start())
    for off in (1, 3, 2):

        @pl.when(z + off < SEC)
        def _():
            mixer_to(off, z).start()
            tensors_to(off, z).start()

    own_piece = pltpu.make_async_copy(
        theta_ref.at[:, :, pl.ds(pl.multiple_of(blk * BS, BS), BS)],
        recv1.at[pl.ds(1 + 2 * blk, 2)],
        local.at[0],
    )
    own_piece.start()
    own_tens = pltpu.make_async_copy(tens_ref, tens.at[z], local.at[1])
    own_tens.start()
    own_w2 = pltpu.make_async_copy(w2_ref, w2.at[z], local.at[2])
    own_w2.start()
    recv1[0] = jnp.zeros((BS, BS), BF16)
    lab_all[me] = lab_ref[...]
    for k in range(2):
        load_env(benv_ref.at[k], left.at[k], envs.at[0, k])

    loop(1, NDEV, lambda off: labels_to(off, lax.rem(me + off, NDEV)).wait_recv())
    total = jnp.zeros((8, BS), jnp.int32)
    for i in range(NBLK):
        total = total + lab_all[2 * i + core]
    inv[...] = total
    to_s0 = pltpu.make_async_copy(lab_all, lab_s, local.at[3])
    to_s0.start()
    to_s1 = pltpu.make_async_copy(inv, inv_s, local.at[4])
    to_s1.start()
    to_s0.wait()
    to_s1.wait()
    own_piece.wait()
    loop(1, NBLK, lambda off: piece_to(off, lax.rem(blk + off, NBLK)).wait_recv())

    def pick(dev):
        for k in range(2):
            label = lab_s[2 * dev + (1 - core), 0, 126 + k]
            for gi in range(2):
                send2[dev, 2 * k + gi] = recv1[inv_s[0, label + 2 * gi]]

    loop(0, NBLK, pick)
    loop(0, NBLK, lambda off: picked_to(off, blk).start())

    own_tens.wait()
    own_w2.wait()

    def stage(sec):
        @pl.when(sec < z)
        def _():
            mixer_to(1, sec).wait_recv()
            tensors_to(1, sec).wait_recv()

        slot = jnp.where(sec < z, 0, 1)

        def site(q):
            i, k = lax.div(q, 2), lax.rem(q, 2)
            env_site(
                tens.at[sec, i, k], w2.at[sec, i], left.at[k], mixed, at, envs.at[slot, k]
            )

        loop(0, 4, site)

    loop(0, z + 1, stage)
    out0 = pltpu.make_async_copy(envs.at[0], envin_ref, local.at[5])
    out1 = pltpu.make_async_copy(envs.at[1], envout_ref, local.at[6])
    out0.start()
    out1.start()

    loop(0, NBLK, lambda off: picked_to(off, lax.rem(blk + off, NBLK)).wait_recv())
    loop(1, NDEV, lambda off: labels_to(off, me).wait_send())
    loop(1, NBLK, lambda off: piece_to(off, blk).wait_send())
    loop(0, NBLK, lambda off: picked_to(off, blk).wait_send())
    for off in (1, 3, 2):

        @pl.when(z + off < SEC)
        def _():
            mixer_to(off, z).wait_send()
            tensors_to(off, z).wait_send()

    out0.wait()
    out1.wait()


def exchange(theta_m, lab_row, tensors, w2, benv):
    hbm = pl.BlockSpec(memory_space=pl.ANY)
    vmem = pl.BlockSpec(memory_space=pltpu.VMEM)
    env_shape = jax.ShapeDtypeStruct((2, WCH, BS, BS), BF16)
    dma = pltpu.SemaphoreType.DMA
    return pl.pallas_call(
        exchange_kernel,
        out_shape=(jax.ShapeDtypeStruct((NBLK, 4, BS, BS), BF16), env_shape, env_shape),
        in_specs=[hbm, vmem, hbm, hbm, vmem],
        out_specs=(hbm, hbm, hbm),
        scratch_shapes=[
            pltpu.VMEM((NDEV + 1, BS, BS), BF16),
            pltpu.VMEM((NBLK, 4, BS, BS), BF16),
            pltpu.VMEM((NDEV, 8, BS), jnp.int32),
            pltpu.VMEM((8, BS), jnp.int32),
            pltpu.SMEM((NDEV, 8, BS), jnp.int32),
            pltpu.SMEM((8, BS), jnp.int32),
            pltpu.VMEM((SEC, 2, 2, PH, BS, BS), BF16),
            pltpu.VMEM((SEC, 2, 80, BS), BF16),
            pltpu.VMEM((2, BS * WP, BS), F32),
            pltpu.VMEM((BS * PH * WCH, BS), F32),
            pltpu.VMEM((BS, PH * BS), BF16),
            pltpu.VMEM((2, 2, WCH, BS, BS), BF16),
            dma((NDEV,)),
            dma((NDEV,)),
            dma((NBLK,)),
            dma((NBLK,)),
            dma((NBLK,)),
            dma((NBLK,)),
            dma((SEC,)),
            dma((SEC,)),
            dma((SEC,)),
            dma((SEC,)),
            dma((8,)),
        ],
        compiler_params=pltpu.CompilerParams(
            collective_id=0, has_side_effects=True, vmem_limit_bytes=VMEM_LIMIT
        ),
        name="exchange_chain",
    )(theta_m, lab_row, tensors, w2, benv)


def build_kron(ops_ref, kron):
    big = (PP * PP, PP)
    rep = (
        lax.div(lax.broadcasted_iota(jnp.int32, big, 0), PP)
        == lax.broadcasted_iota(jnp.int32, big, 1)
    ).astype(F32).astype(BF16)
    wide = (PP, PP * PP)
    rep_t = (
        lax.div(lax.broadcasted_iota(jnp.int32, wide, 1), PP)
        == lax.broadcasted_iota(jnp.int32, wide, 0)
    ).astype(F32).astype(BF16)
    full = (PP * PP, PP * PP)
    same = lax.rem(lax.broadcasted_iota(jnp.int32, full, 0), PP) == lax.rem(
        lax.broadcasted_iota(jnp.int32, full, 1), PP
    )

    def one(w, carry):
        rows = mm(rep, ops_ref[w]).astype(BF16)
        kron[w] = jnp.where(same, mm(rows, rep_t), 0.0).astype(BF16)
        return carry

    lax.fori_loop(0, WCH, one, 0)


def block_product(charge_of, kron, tiles, env_ref, right_ref, mixed, states, acc):
    def pair(wi, carry):
        for e in range(2):
            w = wi * 2 + e
            c = charge_of(w)
            k = kron[w]
            for g in range(4):
                sides = []
                for h in range(2):
                    r0 = (g * 2 + h) * 16
                    sides.append(tiles[c, :, r0 : r0 + 16, :].reshape(PP * 16, BS))
                part = mm(k, jnp.concatenate(sides, axis=1)).astype(BF16)
                for h in range(2):
                    r0 = (g * 2 + h) * 16
                    mixed[:, r0 : r0 + 16, :] = part[:, h * BS : (h + 1) * BS].reshape(PP, 16, BS)
            env = env_ref[w]
            for t in range(0, PP, 2):
                part = mm(env, jnp.concatenate([mixed[t], mixed[t + 1]], axis=1)).astype(BF16)
                states[e, t] = part[:, :BS]
                states[e, t + 1] = part[:, BS:]
        right = right_ref[pl.ds(wi * 2, 2)].reshape(2 * BS, BS)
        for t in range(0, PP, 4):
            both = jnp.concatenate(
                [states[e, t : t + 4].reshape(4 * BS, BS) for e in range(2)], axis=1
            )
            acc[t : t + 4] += mm(both, right).reshape(4, BS, BS)
        return carry

    acc[...] = jnp.zeros_like(acc)
    lax.fori_loop(0, WCH // 2, pair, 0)


def product_kernel(
    charge_ref,
    len_ref,
    energy_ref,
    partner_ref,
    theta_ref,
    env_ref,
    right_ref,
    ops_ref,
    lanczos_ref,
    coef_ref,
    tiles,
    kron,
    mixed,
    states,
    acc,
    mine,
    stats,
    stat_send,
    stat_recv,
    local,
):
    blk = lax.axis_index("blk")
    core = lax.axis_index("charge")
    me = blk * 2 + core
    barrier = pltpu.get_barrier_semaphore()

    def loop(low, high, body):
        def step(i, carry):
            body(i)
            return carry

        lax.fori_loop(low, high, step, 0)

    def greet(off):
        dev = lax.rem(me + off, NDEV)
        pl.semaphore_signal(
            barrier,
            inc=1,
            device_id={"blk": lax.div(dev, 2), "charge": lax.rem(dev, 2)},
            device_id_type=MESH,
        )

    def tile_copy(s):
        out = []
        for k in range(2):
            for gi in range(2):
                out.append(
                    pltpu.make_async_copy(
                        partner_ref.at[s, 2 * k + gi], tiles.at[k, 2 * gi, s], local.at[2 * k + gi, s]
                    )
                )
            out.append(
                pltpu.make_async_copy(
                    theta_ref.at[k, :, pl.ds(pl.multiple_of(s * BS, BS), BS)],
                    tiles.at[k, 1, s],
                    local.at[4 + k, s],
                )
            )
        return out

    loop(0, PP, lambda s: [copy.start() for copy in tile_copy(s)])
    loop(1, NDEV, greet)
    build_kron(ops_ref, kron)
    loop(0, PP, lambda s: [copy.wait() for copy in tile_copy(s)])

    for k in range(2):
        block_product(
            lambda w: charge_ref[w] + 1,
            kron,
            tiles.at[k],
            env_ref.at[k],
            right_ref.at[k],
            mixed,
            states,
            acc.at[k],
        )

    rows = lax.broadcasted_iota(jnp.int32, (BS, BS), 0)
    zero = jnp.zeros((8, BS), F32)

    def fold(x):
        return jnp.sum(x.reshape(16, 8, BS), axis=0)

    def sums_one(t, carry):
        cor, nor = carry
        for k in range(2):
            th = tiles[k, 1, t].astype(F32)
            p = jnp.where(rows < len_ref[k], acc[k, t], 0.0) - energy_ref[k] * th
            acc[k, t] = p
            cor = cor + fold(p * th)
            nor = nor + fold(th * th)
        return cor, nor

    cor, nor = lax.fori_loop(0, PP, sums_one, (zero, zero))

    def everywhere(x):
        return jnp.broadcast_to(
            jnp.sum(jnp.sum(x, axis=0, keepdims=True), axis=1, keepdims=True), (1, BS)
        )

    cor, nor = everywhere(cor), everywhere(nor)
    rho = jnp.where(nor > 0, cor / jnp.where(nor > 0, nor, 1.0), 0.0)

    def sums_two(t, carry):
        sq, cross = carry
        for k in range(2):
            th = tiles[k, 1, t].astype(F32)
            r = acc[k, t] - rho * th
            sq = sq + fold(r * r)
            cross = cross + fold(r * th)
        return sq, cross

    sq, cross = lax.fori_loop(0, PP, sums_two, (zero, zero))
    mine[0:1] = cor
    mine[1:2] = nor
    mine[2:3] = everywhere(sq)
    mine[3:4] = everywhere(cross)
    mine[4:5] = rho
    stats[me] = mine[...]

    def stat_to(off, peer):
        dev = lax.rem(me + off, NDEV)
        return pltpu.make_async_remote_copy(
            src_ref=mine,
            dst_ref=stats.at[me],
            send_sem=stat_send.at[off],
            recv_sem=stat_recv.at[peer],
            device_id={"blk": lax.div(dev, 2), "charge": lax.rem(dev, 2)},
            device_id_type=MESH,
        )

    pl.semaphore_wait(barrier, NDEV - 1)
    loop(1, NDEV, lambda off: stat_to(off, me).start())
    loop(1, NDEV, lambda off: stat_to(off, lax.rem(me + off, NDEV)).wait_recv())

    cor_all = jnp.zeros((1, BS), F32)
    nor_all = jnp.zeros((1, BS), F32)
    for i in range(NDEV):
        cor_all = cor_all + stats[i, 0:1]
        nor_all = nor_all + stats[i, 1:2]
    ray = cor_all / nor_all
    res = jnp.zeros((1, BS), F32)
    for i in range(NDEV):
        gap = stats[i, 4:5] - ray
        res = res + (stats[i, 2:3] + gap * (2.0 * stats[i, 3:4] + gap * stats[i, 1:2]))
    mean_sq = jnp.maximum(res, 0.0) / (NS * BS * M)
    scale = 1.0 / jnp.sqrt(mean_sq + 1e-06)

    def finish(t):
        for k in range(2):
            th = tiles[k, 1, t].astype(F32)
            lanczos_ref[k, :, pl.ds(pl.multiple_of(t * BS, BS), BS)] = (
                (acc[k, t] - ray * th) * scale
            ).astype(BF16)

    loop(0, PP, finish)
    coef_ref[...] = jnp.zeros_like(coef_ref)
    coef_ref[0:1] = ray
    coef_ref[1:2] = jnp.sqrt(mean_sq)
    loop(1, NDEV, lambda off: stat_to(off, me).wait_send())


def product(charges, lens, energy, partner, theta_m, env_in, right, ops_t):
    hbm = pl.BlockSpec(memory_space=pl.ANY)
    vmem = pl.BlockSpec(memory_space=pltpu.VMEM)
    smem = pl.BlockSpec(memory_space=pltpu.SMEM)
    dma = pltpu.SemaphoreType.DMA
    return pl.pallas_call(
        product_kernel,
        out_shape=(
            jax.ShapeDtypeStruct((2, BS, M), BF16),
            jax.ShapeDtypeStruct((8, BS), F32),
        ),
        in_specs=[smem, smem, smem, hbm, hbm, vmem, vmem, vmem],
        out_specs=(vmem, vmem),
        scratch_shapes=[
            pltpu.VMEM((2, 3, PP, BS, BS), BF16),
            pltpu.VMEM((WCH, PP * PP, PP * PP), BF16),
            pltpu.VMEM((PP, BS, BS), BF16),
            pltpu.VMEM((2, PP, BS, BS), BF16),
            pltpu.VMEM((2, PP, BS, BS), F32),
            pltpu.VMEM((8, BS), F32),
            pltpu.VMEM((NDEV, 8, BS), F32),
            dma((NDEV,)),
            dma((NDEV,)),
            dma((6, PP)),
        ],
        compiler_params=pltpu.CompilerParams(
            collective_id=1, has_side_effects=True, vmem_limit_bytes=VMEM_LIMIT
        ),
        name="product_lanczos",
    )(charges, lens, energy, partner, theta_m, env_in, right, ops_t)


def on_device(
    theta,
    boundary_env,
    right_env,
    site_tensors,
    site_mpo,
    bond_ops,
    block_energy,
    sector_charge,
    block_len,
    channel_charge,
):
    labels = sector_charge[0]
    lens = block_len[0]
    row_mask = jnp.arange(BS, dtype=jnp.int32)[None, :] < lens[:, None]
    theta_m = jnp.where(row_mask[:, :, None], theta[0], jnp.zeros((), BF16))
    blk = lax.axis_index("blk")
    lane = jnp.arange(BS, dtype=jnp.int32)
    row = jnp.zeros((BS,), jnp.int32)
    for k in range(2):
        row = row + jnp.where(lane == labels[k] + 1, 2 * blk + k + 1, 0)
        row = row + jnp.where(lane == 126 + k, labels[k], 0)
    lab_row = jnp.broadcast_to(row[None, :], (8, BS))
    w2 = jnp.transpose(site_mpo[0], (0, 3, 2, 4, 1))
    w2 = jnp.pad(w2, ((0, 0), (0, 0), (0, 0), (0, 0), (0, WP - WCH)))
    w2 = w2.reshape(2, PH * WCH, PH * WP)
    w2 = jnp.pad(w2, ((0, 0), (0, 80 - PH * WCH), (0, BS - PH * WP)))
    partner, env_in, env_out = exchange(theta_m, lab_row, site_tensors[0], w2, boundary_env)
    ops_t = jnp.swapaxes(bond_ops[0], 1, 2)
    lanczos, coef = product(
        channel_charge, lens, block_energy[0], partner, theta_m, env_in, right_env[0], ops_t
    )
    return env_out[None], lanczos[None], coef[0:2, 0][None, :]


def solution(mesh):
    return jax.shard_map(
        on_device,
        mesh=mesh,
        in_specs=(
            P("site", ("blk", "charge"), None, None),
            P(("blk", "charge"), None, None, None),
            P("site", ("blk", "charge"), None, None, None),
            P("site", None, ("blk", "charge"), None, None, None),
            P("site", None, None, None, None, None),
            P("site", None, None, None),
            P("site", ("blk", "charge")),
            P("site", ("blk", "charge")),
            P("site", ("blk", "charge")),
            P(),
        ),
        out_specs=(
            P("site", ("blk", "charge"), None, None, None),
            P("site", ("blk", "charge"), None, None),
            P("site", None),
        ),
        check_vma=False,
    )
```

```python
import jax
import jax.numpy as jnp
from jax import lax
from jax.experimental import pallas as pl
from jax.experimental.pallas import tpu as pltpu
from jax.sharding import PartitionSpec as P

BS = 128
PH = 4
WCH = 18
WP = 24
MS = 73
CH = 64
GRP = 6
PRE = 2
PP = 16
M = 2048
NS = 64
SEC = 4
NBLK = 16
NDEV = 32
F32 = jnp.float32
BF16 = jnp.bfloat16
MESH = pl.DeviceIdType.MESH
VMEM_LIMIT = 64 * 1024 * 1024 - 64 * 1024


def mm(a, b):
    return jnp.dot(a, b, preferred_element_type=F32)


def loop(low, high, body):
    def step(i, carry):
        body(i)
        return carry

    lax.fori_loop(low, high, step, 0)


def env_site(a_ref, w_ref, l_ref, m_ref, at_ref, out_ref):
    for t in range(PH):
        at_ref[:, t * BS : (t + 1) * BS] = a_ref[t].T
    a_cat = jnp.concatenate([a_ref[s] for s in range(PH)], axis=1)
    w2 = w_ref[:, : PH * WP]

    def chunk(ci):
        base = pl.multiple_of(ci * (CH * WP), CH * WP)
        left = mm(l_ref[pl.ds(base, CH * WP), :].astype(BF16), a_cat)
        for j in range(0, CH, 2):
            sides = []
            for e in (j, j + 1):
                rows = left[e * WP : (e + 1) * WP]
                sides.append(
                    jnp.concatenate([rows[:, s * BS : (s + 1) * BS] for s in range(PH)], axis=0)
                )
            mixed = mm(w2, jnp.concatenate(sides, axis=1).astype(BF16))
            for e in range(2):
                m_ref[pl.ds((ci * CH + j + e) * MS, PH * WCH), :] = mixed[
                    : PH * WCH, e * BS : (e + 1) * BS
                ]

    loop(0, BS // CH, chunk)

    for v in range(0, WCH, 2):
        sides = []
        for e in range(2):
            sides.append(
                jnp.concatenate(
                    [m_ref[pl.ds(t * WCH + v + e, BS, stride=MS), :] for t in range(PH)], axis=0
                )
            )
        new = mm(at_ref[...], jnp.concatenate(sides, axis=1).astype(BF16))
        for e in range(2):
            one = new[:, e * BS : (e + 1) * BS]
            out_ref[v + e] = one.astype(BF16)
            l_ref[pl.ds(v + e, BS, stride=WP), :] = one


def build_kron(ops_ref, kron):
    big = (PP * PP, PP)
    rep = (
        lax.div(lax.broadcasted_iota(jnp.int32, big, 0), PP)
        == lax.broadcasted_iota(jnp.int32, big, 1)
    ).astype(F32).astype(BF16)
    wide = (PP, PP * PP)
    rep_t = (
        lax.div(lax.broadcasted_iota(jnp.int32, wide, 1), PP)
        == lax.broadcasted_iota(jnp.int32, wide, 0)
    ).astype(F32).astype(BF16)
    full = (PP * PP, PP * PP)
    same = lax.rem(lax.broadcasted_iota(jnp.int32, full, 0), PP) == lax.rem(
        lax.broadcasted_iota(jnp.int32, full, 1), PP
    )

    def one(w):
        rows = lax.dot_general(
            rep, ops_ref[w], (((1,), (1,)), ((), ())), preferred_element_type=F32
        ).astype(BF16)
        kron[w] = jnp.where(same, mm(rows, rep_t), 0.0).astype(BF16)

    loop(0, WCH, one)


def block_product(charge_ref, kron, tiles, env_ref, right_ref, mixed, states, acc):
    def group(wi):
        for e in range(GRP):
            w = wi * GRP + e
            charge = charge_ref[w]
            c = jnp.where(charge == 0, 2, jnp.where(charge < 0, 0, 1))
            big = kron[w]
            for g in range(4):
                sides = []
                for h in range(2):
                    r0 = (g * 2 + h) * 16
                    sides.append(tiles[:, c, r0 : r0 + 16, :].reshape(PP * 16, BS))
                part = mm(big, jnp.concatenate(sides, axis=1)).astype(BF16)
                for h in range(2):
                    r0 = (g * 2 + h) * 16
                    mixed[e, :, r0 : r0 + 16, :] = part[:, h * BS : (h + 1) * BS].reshape(
                        PP, 16, BS
                    )
        for e in range(GRP):
            env = env_ref[wi * GRP + e]
            for t in range(0, PP, 2):
                part = mm(env, jnp.concatenate([mixed[e, t], mixed[e, t + 1]], axis=1))
                part = part.astype(BF16)
                states[e, t] = part[:, :BS]
                states[e, t + 1] = part[:, BS:]
        right = right_ref[pl.ds(wi * GRP, GRP)].reshape(GRP * BS, BS)
        for t in range(0, PP, 4):
            both = jnp.concatenate(
                [states[e, t : t + 4].reshape(4 * BS, BS) for e in range(GRP)], axis=1
            )
            acc[t : t + 4] += mm(both, right).reshape(4, BS, BS)

    acc[...] = jnp.zeros_like(acc)
    loop(0, WCH // GRP, group)


def sweep_kernel(
    charge_ref,
    len_ref,
    energy_ref,
    label_ref,
    theta_ref,
    tens_ref,
    w2_ref,
    benv_ref,
    right_ref,
    ops_ref,
    lanczos_ref,
    coef_ref,
    envout_ref,
    tiles_a,
    tiles_b,
    recv1,
    send2,
    lab_mine,
    lab_all,
    inv,
    lab_s,
    inv_s,
    tens,
    w2,
    left,
    mixer,
    at,
    envs,
    benv,
    right,
    kron,
    mixed,
    states,
    acc,
    mine,
    stats,
    lab_send,
    lab_recv,
    one_send,
    one_recv,
    two_send,
    two_recv,
    ten_send,
    ten_recv,
    w_send,
    w_recv,
    env_send,
    env_recv,
    stat_send,
    stat_recv,
    local,
    tile_sem,
):
    z = lax.axis_index("site")
    blk = lax.axis_index("blk")
    core = lax.axis_index("charge")
    me = blk * 2 + core
    first = lax.div(z, 3)
    other = 1 - first
    tiles = (tiles_a, tiles_b)
    order = (first, other)

    def plane(off):
        dev = lax.rem(me + off, NDEV)
        return {"blk": lax.div(dev, 2), "charge": lax.rem(dev, 2)}

    barrier = pltpu.get_barrier_semaphore()
    loop(
        1,
        NDEV,
        lambda off: pl.semaphore_signal(
            barrier, inc=1, device_id=plane(off), device_id_type=MESH
        ),
    )
    for off in range(1, SEC):
        pl.semaphore_signal(
            barrier, inc=1, device_id={"site": lax.rem(z + off, SEC)}, device_id_type=MESH
        )

    def tile_load(turn, s):
        return pltpu.make_async_copy(
            theta_ref.at[order[turn], :, pl.ds(pl.multiple_of(s * BS, BS), BS)],
            tiles[turn].at[s, 2],
            tile_sem.at[turn, s],
        )

    for turn in range(2):
        loop(0, PP, lambda s: tile_load(turn, s).start())
    loads = [
        pltpu.make_async_copy(benv_ref, benv, local.at[0]),
        pltpu.make_async_copy(tens_ref, tens.at[z], local.at[1]),
        pltpu.make_async_copy(w2_ref, w2.at[z, 0], local.at[2]),
        pltpu.make_async_copy(w2_ref, w2.at[z, 1], local.at[3]),
        pltpu.make_async_copy(right_ref, right, local.at[4]),
    ]
    for copy in loads:
        copy.start()

    lane = lax.broadcasted_iota(jnp.int32, (8, BS), 1)
    row = jnp.zeros((8, BS), jnp.int32)
    for k in range(2):
        row = row + jnp.where(lane == label_ref[0, k] + 1, 2 * blk + k + 1, 0)
        row = row + jnp.where(lane == 126 + k, label_ref[0, k], 0)
    lab_mine[...] = row
    lab_all[me] = row
    recv1[0] = jnp.zeros((BS, BS), BF16)
    rows = lax.broadcasted_iota(jnp.int32, (BS, BS), 0)

    def mask(s):
        for turn in range(2):
            tile_load(turn, s).wait()
            tile = tiles[turn][s, 2].astype(F32)
            tiles[turn][s, 2] = jnp.where(rows < len_ref[0, order[turn]], tile, 0.0).astype(BF16)

    loop(0, PP, mask)
    for turn in range(2):
        recv1[1 + 2 * blk + order[turn]] = tiles[turn][blk, 2]
    pl.semaphore_wait(barrier, NDEV - 1 + SEC - 1)

    def labels_to(off, peer):
        return pltpu.make_async_remote_copy(
            src_ref=lab_mine,
            dst_ref=lab_all.at[me],
            send_sem=lab_send.at[off],
            recv_sem=lab_recv.at[peer],
            device_id=plane(off),
            device_id_type=MESH,
        )

    def piece_to(turn, off, peer):
        dev = lax.rem(blk + off, NBLK)
        return pltpu.make_async_remote_copy(
            src_ref=tiles[turn].at[dev, 2],
            dst_ref=recv1.at[1 + 2 * blk + order[turn]],
            send_sem=one_send.at[turn, off],
            recv_sem=one_recv.at[turn, peer],
            device_id={"blk": dev},
            device_id_type=MESH,
        )

    def picked_to(turn, off, peer):
        dev = lax.rem(blk + off, NBLK)
        return pltpu.make_async_remote_copy(
            src_ref=send2.at[turn, dev],
            dst_ref=tiles[turn].at[blk, pl.ds(0, 2)],
            send_sem=two_send.at[turn, off],
            recv_sem=two_recv.at[turn, peer],
            device_id={"blk": dev, "charge": 1 - core},
            device_id_type=MESH,
        )

    def tensors_to(dst, k, sec):
        return pltpu.make_async_remote_copy(
            src_ref=tens_ref.at[:, k],
            dst_ref=tens.at[z, :, k],
            send_sem=ten_send.at[dst, k],
            recv_sem=ten_recv.at[sec, k],
            device_id={"site": dst},
            device_id_type=MESH,
        )

    def mixer_to(dst, k, sec):
        return pltpu.make_async_remote_copy(
            src_ref=w2_ref,
            dst_ref=w2.at[z, k],
            send_sem=w_send.at[dst, k],
            recv_sem=w_recv.at[sec, k],
            device_id={"site": dst},
            device_id_type=MESH,
        )

    routes = (
        (0, 1, 0), (0, 3, 1), (0, 1, 1), (0, 2, 0),
        (1, 2, 0), (1, 3, 1), (2, 3, 1), (3, 2, 0),
    )

    loop(1, NDEV, lambda off: labels_to(off, me).start())
    for src, dst, k in routes:

        @pl.when(z == src)
        def _():
            mixer_to(dst, k, src).start()
            tensors_to(dst, k, src).start()

    for turn in range(2):
        loop(1, NBLK, lambda off: piece_to(turn, off, blk).start())

    build_kron(ops_ref, kron)
    for copy in loads:
        copy.wait()
    for k in range(2):

        @pl.when((z < 2) | (z == k + 2))
        def _():
            left[k] = jnp.zeros((BS * WP, BS), F32)

            def one(v):
                left[k, pl.ds(v, BS, stride=WP), :] = benv[k, v].astype(F32)

            loop(0, WCH, one)

        @pl.when(z == 0)
        def _():
            envs[0, k] = benv[k]

    def send_picked():
        loop(1, NDEV, lambda off: labels_to(off, lax.rem(me + off, NDEV)).wait_recv())
        total = jnp.zeros((8, BS), jnp.int32)
        for i in range(NBLK):
            total = total + lab_all[2 * i + core]
        inv[...] = total
        to_s0 = pltpu.make_async_copy(lab_all, lab_s, local.at[5])
        to_s0.start()
        to_s1 = pltpu.make_async_copy(inv, inv_s, local.at[6])
        to_s1.start()
        to_s0.wait()
        to_s1.wait()
        for turn in range(2):
            loop(1, NBLK, lambda off: piece_to(turn, off, lax.rem(blk + off, NBLK)).wait_recv())
        for turn in range(2):

            def pick(dev):
                label = lab_s[2 * dev + (1 - core), 0, 126 + order[turn]]
                for gi in range(2):
                    send2[turn, dev, gi] = recv1[inv_s[0, label + 2 * gi]]

            loop(0, NBLK, pick)
            loop(0, NBLK, lambda off: picked_to(turn, off, blk).start())

    def env_to(slot, dst_slot, k, dst, which):
        return pltpu.make_async_remote_copy(
            src_ref=envs.at[slot, k],
            dst_ref=envs.at[dst_slot, k],
            send_sem=env_send.at[which],
            recv_sem=env_recv.at[which],
            device_id={"site": dst},
            device_id_type=MESH,
        )

    env_routes = ((2, 5, 1, 0, 0, 3, 0), (2, 7, 2, 1, 0, 3, 1), (3, 3, 2, 0, 1, 2, 0), (3, 5, 0, 1, 1, 2, 1))

    def site(q):
        unit, i = lax.div(q, 2), lax.rem(q, 2)
        sec = jnp.where(z < 2, lax.div(unit, 2), unit)
        k = jnp.where(z < 2, lax.rem(unit, 2), z - 2)

        @pl.when(q == PRE)
        def _():
            send_picked()

        @pl.when((i == 0) & (sec != z))
        def _():
            mixer_to(0, k, sec).wait_recv()
            tensors_to(0, k, sec).wait_recv()

        slot = jnp.where(sec == z, 1, jnp.where(sec < z, 0, 2))
        slot = jnp.where((z == 3) & (sec == 1), 2, slot)
        env_site(tens.at[sec, i, k], w2.at[sec, k, i], left.at[k], mixer, at, envs.at[slot, k])
        for src, when, slot_at, dst_slot, kk, dst, which in env_routes:

            @pl.when((z == src) & (q == when))
            def _():
                env_to(slot_at, dst_slot, kk, dst, which).start()

    loop(0, jnp.where(z == 0, 4, 8), site)

    for turn in range(2):
        k = order[turn]
        loop(0, NBLK, lambda off: picked_to(turn, off, lax.rem(blk + off, NBLK)).wait_recv())
        if turn:

            @pl.when(z >= 2)
            def _():
                env_to(0, 0, 0, 0, 0).wait_recv()

        block_product(
            charge_ref, kron, tiles[turn], envs.at[0, k], right.at[k], mixed, states, acc.at[turn]
        )

    @pl.when(z >= 2)
    def _():
        env_to(0, 0, 0, 0, 1).wait_recv()

    env_store = pltpu.make_async_copy(envs.at[1], envout_ref, local.at[7])
    env_store.start()

    zero = jnp.zeros((8, BS), F32)

    def fold(x):
        return jnp.sum(x.reshape(16, 8, BS), axis=0)

    def sums_one(t, carry):
        cor, nor = carry
        for turn in range(2):
            k = order[turn]
            th = tiles[turn][t, 2].astype(F32)
            p = jnp.where(rows < len_ref[0, k], acc[turn, t], 0.0) - energy_ref[0, k] * th
            acc[turn, t] = p
            cor = cor + fold(p * th)
            nor = nor + fold(th * th)
        return cor, nor

    cor, nor = lax.fori_loop(0, PP, sums_one, (zero, zero))

    def everywhere(x):
        return jnp.broadcast_to(
            jnp.sum(jnp.sum(x, axis=0, keepdims=True), axis=1, keepdims=True), (1, BS)
        )

    cor, nor = everywhere(cor), everywhere(nor)
    rho = jnp.where(nor > 0, cor / jnp.where(nor > 0, nor, 1.0), 0.0)

    def sums_two(t, carry):
        sq, cross = carry
        for turn in range(2):
            th = tiles[turn][t, 2].astype(F32)
            r = acc[turn, t] - rho * th
            sq = sq + fold(r * r)
            cross = cross + fold(r * th)
        return sq, cross

    sq, cross = lax.fori_loop(0, PP, sums_two, (zero, zero))
    mine[...] = jnp.concatenate(
        [cor, nor, everywhere(sq), everywhere(cross), rho, jnp.zeros((3, BS), F32)], axis=0
    )
    stats[me] = mine[...]

    def stat_to(off, peer):
        return pltpu.make_async_remote_copy(
            src_ref=mine,
            dst_ref=stats.at[me],
            send_sem=stat_send.at[off],
            recv_sem=stat_recv.at[peer],
            device_id=plane(off),
            device_id_type=MESH,
        )

    loop(1, NDEV, lambda off: stat_to(off, me).start())
    loop(1, NDEV, lambda off: labels_to(off, me).wait_send())
    for turn in range(2):
        loop(1, NBLK, lambda off: piece_to(turn, off, blk).wait_send())
        loop(0, NBLK, lambda off: picked_to(turn, off, blk).wait_send())
    for src, dst, k in routes:

        @pl.when(z == src)
        def _():
            mixer_to(dst, k, src).wait_send()
            tensors_to(dst, k, src).wait_send()

    for src, when, slot_at, dst_slot, kk, dst, which in env_routes:

        @pl.when(z == src)
        def _():
            env_to(slot_at, dst_slot, kk, dst, which).wait_send()

    loop(1, NDEV, lambda off: stat_to(off, lax.rem(me + off, NDEV)).wait_recv())

    cor_all = jnp.zeros((1, BS), F32)
    nor_all = jnp.zeros((1, BS), F32)
    for i in range(NDEV):
        cor_all = cor_all + stats[i, 0:1]
        nor_all = nor_all + stats[i, 1:2]
    ray = cor_all / nor_all
    res = jnp.zeros((1, BS), F32)
    for i in range(NDEV):
        gap = stats[i, 4:5] - ray
        res = res + (stats[i, 2:3] + gap * (2.0 * stats[i, 3:4] + gap * stats[i, 1:2]))
    mean_sq = jnp.maximum(res, 0.0) / (NS * BS * M)
    scale = 1.0 / jnp.sqrt(mean_sq + 1e-06)

    def finish(t):
        for turn in range(2):
            th = tiles[turn][t, 2].astype(F32)
            lanczos_ref[order[turn], :, pl.ds(pl.multiple_of(t * BS, BS), BS)] = (
                (acc[turn, t] - ray * th) * scale
            ).astype(BF16)

    loop(0, PP, finish)
    coef_ref[...] = jnp.concatenate(
        [ray, jnp.sqrt(mean_sq), jnp.zeros((6, BS), F32)], axis=0
    )
    loop(1, NDEV, lambda off: stat_to(off, me).wait_send())
    env_store.wait()


def sweep(charges, lens, energy, labels, theta, tensors, w2, benv, right, ops):
    hbm = pl.BlockSpec(memory_space=pl.ANY)
    vmem = pl.BlockSpec(memory_space=pltpu.VMEM)
    smem = pl.BlockSpec(memory_space=pltpu.SMEM)
    dma = pltpu.SemaphoreType.DMA
    return pl.pallas_call(
        sweep_kernel,
        out_shape=(
            jax.ShapeDtypeStruct((2, BS, M), BF16),
            jax.ShapeDtypeStruct((8, BS), F32),
            jax.ShapeDtypeStruct((2, WCH, BS, BS), BF16),
        ),
        in_specs=[smem] * 4 + [hbm] * 5 + [vmem],
        out_specs=(vmem, vmem, hbm),
        scratch_shapes=[
            pltpu.VMEM((PP, 3, BS, BS), BF16),
            pltpu.VMEM((PP, 3, BS, BS), BF16),
            pltpu.VMEM((NDEV + 1, BS, BS), BF16),
            pltpu.VMEM((2, NBLK, 2, BS, BS), BF16),
            pltpu.VMEM((8, BS), jnp.int32),
            pltpu.VMEM((NDEV, 8, BS), jnp.int32),
            pltpu.VMEM((8, BS), jnp.int32),
            pltpu.SMEM((NDEV, 8, BS), jnp.int32),
            pltpu.SMEM((8, BS), jnp.int32),
            pltpu.VMEM((SEC, 2, 2, PH, BS, BS), BF16),
            pltpu.VMEM((SEC, 2, 2, 80, BS), BF16),
            pltpu.VMEM((2, BS * WP, BS), F32),
            pltpu.VMEM((BS * MS, BS), F32),
            pltpu.VMEM((BS, PH * BS), BF16),
            pltpu.VMEM((3, 2, WCH, BS, BS), BF16),
            pltpu.VMEM((2, WCH, BS, BS), BF16),
            pltpu.VMEM((2, WCH, BS, BS), BF16),
            pltpu.VMEM((WCH, PP * PP, PP * PP), BF16),
            pltpu.VMEM((GRP, PP, BS, BS), BF16),
            pltpu.VMEM((GRP, PP, BS, BS), BF16),
            pltpu.VMEM((2, PP, BS, BS), F32),
            pltpu.VMEM((8, BS), F32),
            pltpu.VMEM((NDEV, 8, BS), F32),
            dma((NDEV,)),
            dma((NDEV,)),
            dma((2, NBLK)),
            dma((2, NBLK)),
            dma((2, NBLK)),
            dma((2, NBLK)),
            dma((SEC, 2)),
            dma((SEC, 2)),
            dma((SEC, 2)),
            dma((SEC, 2)),
            dma((2,)),
            dma((2,)),
            dma((NDEV,)),
            dma((NDEV,)),
            dma((8,)),
            dma((2, PP)),
        ],
        compiler_params=pltpu.CompilerParams(
            collective_id=0, has_side_effects=True, vmem_limit_bytes=VMEM_LIMIT
        ),
        name="sweep",
    )(charges, lens, energy, labels, theta, tensors, w2, benv, right, ops)


def on_device(
    theta,
    boundary_env,
    right_env,
    site_tensors,
    site_mpo,
    bond_ops,
    block_energy,
    sector_charge,
    block_len,
    channel_charge,
):
    w2 = jnp.transpose(site_mpo[0], (0, 3, 2, 4, 1))
    w2 = jnp.pad(w2, ((0, 0), (0, 0), (0, 0), (0, 0), (0, WP - WCH)))
    w2 = w2.reshape(2, PH * WCH, PH * WP)
    w2 = jnp.pad(w2, ((0, 0), (0, 80 - PH * WCH), (0, BS - PH * WP)))
    lanczos, coef, env_out = sweep(
        channel_charge,
        block_len,
        block_energy,
        sector_charge,
        theta[0],
        site_tensors[0],
        w2,
        boundary_env,
        right_env[0],
        bond_ops[0],
    )
    return env_out[None], lanczos[None], coef[0:2, 0][None, :]


def solution(mesh):
    return jax.shard_map(
        on_device,
        mesh=mesh,
        in_specs=(
            P("site", ("blk", "charge"), None, None),
            P(("blk", "charge"), None, None, None),
            P("site", ("blk", "charge"), None, None, None),
            P("site", None, ("blk", "charge"), None, None, None),
            P("site", None, None, None, None, None),
            P("site", None, None, None),
            P("site", ("blk", "charge")),
            P("site", ("blk", "charge")),
            P("site", ("blk", "charge")),
            P(),
        ),
        out_specs=(
            P("site", ("blk", "charge"), None, None, None),
            P("site", ("blk", "charge"), None, None),
            P("site", None),
        ),
        check_vma=False,
    )
```

```python
import jax
import jax.numpy as jnp
from jax import lax
from jax.experimental import pallas as pl
from jax.experimental.pallas import tpu as pltpu
from jax.sharding import PartitionSpec as P

BS = 128
PH = 4
WCH = 18
WP = 24
MS = 73
CH = 64
GRP = 6
PRE = 0
PP = 16
M = 2048
NS = 64
SEC = 4
NBLK = 16
NDEV = 32
SIDE = 4
STEPS = (
    (1, 1), (3, 3), (2, 2), (1, 3), (3, 1), (2, 0), (0, 2), (1, 2),
    (3, 2), (2, 1), (2, 3), (1, 0), (3, 0), (0, 1), (0, 3),
)
F32 = jnp.float32
BF16 = jnp.bfloat16
MESH = pl.DeviceIdType.MESH
VMEM_LIMIT = 64 * 1024 * 1024 - 64 * 1024


def mm(a, b):
    return jnp.dot(a, b, preferred_element_type=F32)


def loop(low, high, body):
    def step(i, carry):
        body(i)
        return carry

    lax.fori_loop(low, high, step, 0)


def env_site(a_ref, w_ref, l_ref, m_ref, at_ref, out_ref):
    for t in range(PH):
        at_ref[:, t * BS : (t + 1) * BS] = a_ref[t].T
    a_cat = jnp.concatenate([a_ref[s] for s in range(PH)], axis=1)
    w2 = w_ref[:, : PH * WP]

    def chunk(ci):
        base = pl.multiple_of(ci * (CH * WP), CH * WP)
        left = mm(l_ref[pl.ds(base, CH * WP), :].astype(BF16), a_cat)
        for j in range(0, CH, 2):
            sides = []
            for e in (j, j + 1):
                rows = left[e * WP : (e + 1) * WP]
                sides.append(
                    jnp.concatenate([rows[:, s * BS : (s + 1) * BS] for s in range(PH)], axis=0)
                )
            mixed = mm(w2, jnp.concatenate(sides, axis=1).astype(BF16))
            for e in range(2):
                m_ref[pl.ds((ci * CH + j + e) * MS, PH * WCH), :] = mixed[
                    : PH * WCH, e * BS : (e + 1) * BS
                ]

    loop(0, BS // CH, chunk)

    for v in range(0, WCH, 2):
        sides = []
        for e in range(2):
            sides.append(
                jnp.concatenate(
                    [m_ref[pl.ds(t * WCH + v + e, BS, stride=MS), :] for t in range(PH)], axis=0
                )
            )
        new = mm(at_ref[...], jnp.concatenate(sides, axis=1).astype(BF16))
        for e in range(2):
            one = new[:, e * BS : (e + 1) * BS]
            out_ref[v + e] = one.astype(BF16)
            l_ref[pl.ds(v + e, BS, stride=WP), :] = one


def build_kron(ops_ref, kron):
    big = (PP * PP, PP)
    rep = (
        lax.div(lax.broadcasted_iota(jnp.int32, big, 0), PP)
        == lax.broadcasted_iota(jnp.int32, big, 1)
    ).astype(F32).astype(BF16)
    wide = (PP, PP * PP)
    rep_t = (
        lax.div(lax.broadcasted_iota(jnp.int32, wide, 1), PP)
        == lax.broadcasted_iota(jnp.int32, wide, 0)
    ).astype(F32).astype(BF16)
    full = (PP * PP, PP * PP)
    same = lax.rem(lax.broadcasted_iota(jnp.int32, full, 0), PP) == lax.rem(
        lax.broadcasted_iota(jnp.int32, full, 1), PP
    )

    def one(w):
        rows = lax.dot_general(
            rep, ops_ref[w], (((1,), (1,)), ((), ())), preferred_element_type=F32
        ).astype(BF16)
        kron[w] = jnp.where(same, mm(rows, rep_t), 0.0).astype(BF16)

    loop(0, WCH, one)


def block_product(charge_ref, kron, tiles, env_ref, right_ref, mixed, states, acc):
    def group(wi):
        for e in range(GRP):
            w = wi * GRP + e
            charge = charge_ref[w]
            c = jnp.where(charge == 0, 2, jnp.where(charge < 0, 0, 1))
            big = kron[w]
            for g in range(4):
                sides = []
                for h in range(2):
                    r0 = (g * 2 + h) * 16
                    sides.append(tiles[:, c, r0 : r0 + 16, :].reshape(PP * 16, BS))
                part = mm(big, jnp.concatenate(sides, axis=1)).astype(BF16)
                for h in range(2):
                    r0 = (g * 2 + h) * 16
                    mixed[e, :, r0 : r0 + 16, :] = part[:, h * BS : (h + 1) * BS].reshape(
                        PP, 16, BS
                    )
        for e in range(GRP):
            env = env_ref[wi * GRP + e]
            for t in range(0, PP, 2):
                part = mm(env, jnp.concatenate([mixed[e, t], mixed[e, t + 1]], axis=1))
                part = part.astype(BF16)
                states[e, t] = part[:, :BS]
                states[e, t + 1] = part[:, BS:]
        right = right_ref[pl.ds(wi * GRP, GRP)].reshape(GRP * BS, BS)
        for t in range(0, PP, 4):
            both = jnp.concatenate(
                [states[e, t : t + 4].reshape(4 * BS, BS) for e in range(GRP)], axis=1
            )
            acc[t : t + 4] += mm(both, right).reshape(4, BS, BS)

    acc[...] = jnp.zeros_like(acc)
    loop(0, WCH // GRP, group)


def sweep_kernel(
    charge_ref,
    len_ref,
    energy_ref,
    label_ref,
    theta_ref,
    tens_ref,
    w2_ref,
    benv_ref,
    right_ref,
    ops_ref,
    lanczos_ref,
    coef_ref,
    envout_ref,
    tiles_a,
    tiles_b,
    recv1,
    send2,
    lab_mine,
    lab_all,
    inv,
    lab_s,
    inv_s,
    tens,
    w2,
    left,
    mixer,
    at,
    envs,
    benv,
    right,
    kron,
    mixed,
    states,
    acc,
    mine,
    stats,
    lab_send,
    lab_recv,
    one_send,
    one_recv,
    two_send,
    two_recv,
    ten_send,
    ten_recv,
    w_send,
    w_recv,
    env_send,
    env_recv,
    stat_send,
    stat_recv,
    local,
    tile_sem,
):
    z = lax.axis_index("site")
    blk = lax.axis_index("blk")
    core = lax.axis_index("charge")
    me = blk * 2 + core
    first = lax.div(z, 3)
    other = 1 - first
    tiles = (tiles_a, tiles_b)
    order = (first, other)

    def ahead(dx, dy):
        return lax.rem(lax.div(blk, SIDE) + dx, SIDE) * SIDE + lax.rem(lax.rem(blk, SIDE) + dy, SIDE)

    def plane(off):
        dev = lax.rem(me + off, NDEV)
        return {"blk": lax.div(dev, 2), "charge": lax.rem(dev, 2)}

    barrier = pltpu.get_barrier_semaphore()
    loop(
        1,
        NDEV,
        lambda off: pl.semaphore_signal(
            barrier, inc=1, device_id=plane(off), device_id_type=MESH
        ),
    )
    for off in range(1, SEC):
        pl.semaphore_signal(
            barrier, inc=1, device_id={"site": lax.rem(z + off, SEC)}, device_id_type=MESH
        )

    def tile_load(turn, s):
        return pltpu.make_async_copy(
            theta_ref.at[order[turn], :, pl.ds(pl.multiple_of(s * BS, BS), BS)],
            tiles[turn].at[s, 2],
            tile_sem.at[turn, s],
        )

    for turn in range(2):
        loop(0, PP, lambda s: tile_load(turn, s).start())
    loads = [
        pltpu.make_async_copy(benv_ref, benv, local.at[0]),
        pltpu.make_async_copy(tens_ref, tens.at[z], local.at[1]),
        pltpu.make_async_copy(w2_ref, w2.at[z, 0], local.at[2]),
        pltpu.make_async_copy(w2_ref, w2.at[z, 1], local.at[3]),
        pltpu.make_async_copy(right_ref, right, local.at[4]),
    ]
    for copy in loads:
        copy.start()

    lane = lax.broadcasted_iota(jnp.int32, (8, BS), 1)
    row = jnp.zeros((8, BS), jnp.int32)
    for k in range(2):
        row = row + jnp.where(lane == label_ref[0, k] + 1, 2 * blk + k + 1, 0)
        row = row + jnp.where(lane == 126 + k, label_ref[0, k], 0)
    lab_mine[...] = row
    lab_all[me] = row
    recv1[0] = jnp.zeros((BS, BS), BF16)
    rows = lax.broadcasted_iota(jnp.int32, (BS, BS), 0)

    def mask(s):
        for turn in range(2):
            tile_load(turn, s).wait()
            tile = tiles[turn][s, 2].astype(F32)
            tiles[turn][s, 2] = jnp.where(rows < len_ref[0, order[turn]], tile, 0.0).astype(BF16)

    loop(0, PP, mask)
    for turn in range(2):
        recv1[1 + 2 * blk + order[turn]] = tiles[turn][blk, 2]
    pl.semaphore_wait(barrier, NDEV - 1 + SEC - 1)

    def labels_to(off, peer):
        return pltpu.make_async_remote_copy(
            src_ref=lab_mine,
            dst_ref=lab_all.at[me],
            send_sem=lab_send.at[off],
            recv_sem=lab_recv.at[peer],
            device_id=plane(off),
            device_id_type=MESH,
        )

    def piece_to(turn, step, dev, peer):
        return pltpu.make_async_remote_copy(
            src_ref=tiles[turn].at[dev, 2],
            dst_ref=recv1.at[1 + 2 * blk + order[turn]],
            send_sem=one_send.at[turn, step],
            recv_sem=one_recv.at[turn, peer],
            device_id={"blk": dev},
            device_id_type=MESH,
        )

    def picked_to(turn, step, dev, peer):
        return pltpu.make_async_remote_copy(
            src_ref=send2.at[turn, dev],
            dst_ref=tiles[turn].at[blk, pl.ds(0, 2)],
            send_sem=two_send.at[turn, step],
            recv_sem=two_recv.at[turn, peer],
            device_id={"blk": dev, "charge": 1 - core},
            device_id_type=MESH,
        )

    def tensors_to(dst, k, sec):
        return pltpu.make_async_remote_copy(
            src_ref=tens_ref.at[:, k],
            dst_ref=tens.at[z, :, k],
            send_sem=ten_send.at[dst, k],
            recv_sem=ten_recv.at[sec, k],
            device_id={"site": dst},
            device_id_type=MESH,
        )

    def mixer_to(dst, k, sec):
        return pltpu.make_async_remote_copy(
            src_ref=w2_ref,
            dst_ref=w2.at[z, k],
            send_sem=w_send.at[dst, k],
            recv_sem=w_recv.at[sec, k],
            device_id={"site": dst},
            device_id_type=MESH,
        )

    routes = (
        (0, 3, 1), (0, 2, 0), (0, 1, 0), (0, 1, 1),
        (1, 3, 1), (1, 2, 0), (2, 3, 1),
    )

    loop(1, NDEV, lambda off: labels_to(off, me).start())
    for src, dst, k in routes:

        @pl.when(z == src)
        def _():
            mixer_to(dst, k, src).start()
            tensors_to(dst, k, src).start()

    for turn in range(2):
        for step, (dx, dy) in enumerate(STEPS):
            piece_to(turn, step, ahead(dx, dy), blk).start()

    build_kron(ops_ref, kron)
    for copy in loads:
        copy.wait()

    def load_left(k, env_ref):
        left[k] = jnp.zeros((BS * WP, BS), F32)

        def one(v):
            left[k, pl.ds(v, BS, stride=WP), :] = env_ref[v].astype(F32)

        loop(0, WCH, one)

    for k in range(2):

        @pl.when((z < 2) | (z == k + 2))
        def _():
            load_left(k, benv.at[k])

        @pl.when(z == 0)
        def _():
            envs[0, k] = benv[k]

    def send_picked():
        loop(1, NDEV, lambda off: labels_to(off, lax.rem(me + off, NDEV)).wait_recv())
        total = jnp.zeros((8, BS), jnp.int32)
        for i in range(NBLK):
            total = total + lab_all[2 * i + core]
        inv[...] = total
        to_s0 = pltpu.make_async_copy(lab_all, lab_s, local.at[5])
        to_s0.start()
        to_s1 = pltpu.make_async_copy(inv, inv_s, local.at[6])
        to_s1.start()
        to_s0.wait()
        to_s1.wait()
        for turn in range(2):
            loop(1, NBLK, lambda i: piece_to(turn, 0, 0, lax.rem(blk + i, NBLK)).wait_recv())
        for turn in range(2):

            def pick(dev):
                label = lab_s[2 * dev + (1 - core), 0, 126 + order[turn]]
                for gi in range(2):
                    send2[turn, dev, gi] = recv1[inv_s[0, label + 2 * gi]]

            loop(0, NBLK, pick)
            for step, (dx, dy) in enumerate(((0, 0),) + STEPS):
                picked_to(turn, step, ahead(dx, dy), blk).start()

    def env_to(slot, k, dst):
        return pltpu.make_async_remote_copy(
            src_ref=envs.at[slot, k],
            dst_ref=envs.at[0, k],
            send_sem=env_send,
            recv_sem=env_recv,
            device_id={"site": dst},
            device_id_type=MESH,
        )

    env_routes = ((2, 5, 1, 0, 3), (3, 3, 2, 1, 2))

    def site(q):
        unit, i = lax.div(q, 2), lax.rem(q, 2)
        sec = jnp.where(z < 2, lax.div(unit, 2), unit)
        k = jnp.where(z < 2, lax.rem(unit, 2), z - 2)

        @pl.when(q == PRE)
        def _():
            send_picked()

        @pl.when((i == 0) & (sec != z))
        def _():
            mixer_to(0, k, sec).wait_recv()
            tensors_to(0, k, sec).wait_recv()

        slot = jnp.where(sec == z, 1, 0)
        slot = jnp.where((z == 3) & (sec == 1), 2, slot)
        env_site(tens.at[sec, i, k], w2.at[sec, k, i], left.at[k], mixer, at, envs.at[slot, k])
        for src, when, slot_at, kk, dst in env_routes:

            @pl.when((z == src) & (q == when))
            def _():
                env_to(slot_at, kk, dst).start()

    loop(0, jnp.where(z == 0, 4, jnp.where(z == 2, 6, 8)), site)

    def late_sites():
        env_to(0, 0, 0).wait_recv()
        load_left(other, envs.at[0, other])

        def late(i):
            env_site(
                tens.at[z, i, other], w2.at[z, other, i], left.at[other], mixer, at, envs.at[1, other]
            )

        loop(0, 2, late)

    for turn in range(2):
        k = order[turn]
        if turn:
            pl.when(z >= 2)(late_sites)
            env_store = pltpu.make_async_copy(envs.at[1], envout_ref, local.at[7])
            env_store.start()
        loop(0, NBLK, lambda i: picked_to(turn, 0, 0, lax.rem(blk + i, NBLK)).wait_recv())
        block_product(
            charge_ref, kron, tiles[turn], envs.at[0, k], right.at[k], mixed, states, acc.at[turn]
        )

    zero = jnp.zeros((8, BS), F32)

    def fold(x):
        return jnp.sum(x.reshape(16, 8, BS), axis=0)

    def sums_one(t, carry):
        cor, nor = carry
        for turn in range(2):
            k = order[turn]
            th = tiles[turn][t, 2].astype(F32)
            p = jnp.where(rows < len_ref[0, k], acc[turn, t], 0.0) - energy_ref[0, k] * th
            acc[turn, t] = p
            cor = cor + fold(p * th)
            nor = nor + fold(th * th)
        return cor, nor

    cor, nor = lax.fori_loop(0, PP, sums_one, (zero, zero))

    def everywhere(x):
        return jnp.broadcast_to(
            jnp.sum(jnp.sum(x, axis=0, keepdims=True), axis=1, keepdims=True), (1, BS)
        )

    cor, nor = everywhere(cor), everywhere(nor)
    rho = jnp.where(nor > 0, cor / jnp.where(nor > 0, nor, 1.0), 0.0)

    def sums_two(t, carry):
        sq, cross = carry
        for turn in range(2):
            th = tiles[turn][t, 2].astype(F32)
            r = acc[turn, t] - rho * th
            sq = sq + fold(r * r)
            cross = cross + fold(r * th)
        return sq, cross

    sq, cross = lax.fori_loop(0, PP, sums_two, (zero, zero))
    mine[...] = jnp.concatenate(
        [cor, nor, everywhere(sq), everywhere(cross), rho, jnp.zeros((3, BS), F32)], axis=0
    )
    stats[me] = mine[...]

    def stat_to(off, peer):
        return pltpu.make_async_remote_copy(
            src_ref=mine,
            dst_ref=stats.at[me],
            send_sem=stat_send.at[off],
            recv_sem=stat_recv.at[peer],
            device_id=plane(off),
            device_id_type=MESH,
        )

    loop(1, NDEV, lambda off: stat_to(off, me).start())
    loop(1, NDEV, lambda off: labels_to(off, me).wait_send())
    for turn in range(2):
        loop(0, NBLK - 1, lambda step: piece_to(turn, step, 0, blk).wait_send())
        loop(0, NBLK, lambda step: picked_to(turn, step, 0, blk).wait_send())
    for src, dst, k in routes:

        @pl.when(z == src)
        def _():
            mixer_to(dst, k, src).wait_send()
            tensors_to(dst, k, src).wait_send()

    for src, when, slot_at, kk, dst in env_routes:

        @pl.when(z == src)
        def _():
            env_to(slot_at, kk, dst).wait_send()

    loop(1, NDEV, lambda off: stat_to(off, lax.rem(me + off, NDEV)).wait_recv())

    cor_all = jnp.zeros((1, BS), F32)
    nor_all = jnp.zeros((1, BS), F32)
    for i in range(NDEV):
        cor_all = cor_all + stats[i, 0:1]
        nor_all = nor_all + stats[i, 1:2]
    ray = cor_all / nor_all
    res = jnp.zeros((1, BS), F32)
    for i in range(NDEV):
        gap = stats[i, 4:5] - ray
        res = res + (stats[i, 2:3] + gap * (2.0 * stats[i, 3:4] + gap * stats[i, 1:2]))
    mean_sq = jnp.maximum(res, 0.0) / (NS * BS * M)
    scale = 1.0 / jnp.sqrt(mean_sq + 1e-06)

    def finish(t):
        for turn in range(2):
            th = tiles[turn][t, 2].astype(F32)
            lanczos_ref[order[turn], :, pl.ds(pl.multiple_of(t * BS, BS), BS)] = (
                (acc[turn, t] - ray * th) * scale
            ).astype(BF16)

    loop(0, PP, finish)
    coef_ref[0, 0] = ray[0, 0]
    coef_ref[0, 1] = jnp.sqrt(mean_sq)[0, 0]
    loop(1, NDEV, lambda off: stat_to(off, me).wait_send())
    env_store.wait()


def sweep(charges, lens, energy, labels, theta, tensors, w2, benv, right, ops):
    hbm = pl.BlockSpec(memory_space=pl.ANY)
    vmem = pl.BlockSpec(memory_space=pltpu.VMEM)
    smem = pl.BlockSpec(memory_space=pltpu.SMEM)
    dma = pltpu.SemaphoreType.DMA
    return pl.pallas_call(
        sweep_kernel,
        out_shape=(
            jax.ShapeDtypeStruct((2, BS, M), BF16),
            jax.ShapeDtypeStruct((1, 2), F32),
            jax.ShapeDtypeStruct((2, WCH, BS, BS), BF16),
        ),
        in_specs=[smem] * 4 + [hbm] * 5 + [vmem],
        out_specs=(vmem, smem, hbm),
        scratch_shapes=[
            pltpu.VMEM((PP, 3, BS, BS), BF16),
            pltpu.VMEM((PP, 3, BS, BS), BF16),
            pltpu.VMEM((NDEV + 1, BS, BS), BF16),
            pltpu.VMEM((2, NBLK, 2, BS, BS), BF16),
            pltpu.VMEM((8, BS), jnp.int32),
            pltpu.VMEM((NDEV, 8, BS), jnp.int32),
            pltpu.VMEM((8, BS), jnp.int32),
            pltpu.SMEM((NDEV, 8, BS), jnp.int32),
            pltpu.SMEM((8, BS), jnp.int32),
            pltpu.VMEM((SEC, 2, 2, PH, BS, BS), BF16),
            pltpu.VMEM((SEC, 2, 2, 80, BS), BF16),
            pltpu.VMEM((2, BS * WP, BS), F32),
            pltpu.VMEM((BS * MS, BS), F32),
            pltpu.VMEM((BS, PH * BS), BF16),
            pltpu.VMEM((3, 2, WCH, BS, BS), BF16),
            pltpu.VMEM((2, WCH, BS, BS), BF16),
            pltpu.VMEM((2, WCH, BS, BS), BF16),
            pltpu.VMEM((WCH, PP * PP, PP * PP), BF16),
            pltpu.VMEM((GRP, PP, BS, BS), BF16),
            pltpu.VMEM((GRP, PP, BS, BS), BF16),
            pltpu.VMEM((2, PP, BS, BS), F32),
            pltpu.VMEM((8, BS), F32),
            pltpu.VMEM((NDEV, 8, BS), F32),
            dma((NDEV,)),
            dma((NDEV,)),
            dma((2, NBLK)),
            dma((2, NBLK)),
            dma((2, NBLK)),
            dma((2, NBLK)),
            dma((SEC, 2)),
            dma((SEC, 2)),
            dma((SEC, 2)),
            dma((SEC, 2)),
            dma,
            dma,
            dma((NDEV,)),
            dma((NDEV,)),
            dma((8,)),
            dma((2, PP)),
        ],
        compiler_params=pltpu.CompilerParams(
            collective_id=0, has_side_effects=True, vmem_limit_bytes=VMEM_LIMIT
        ),
        name="sweep",
    )(charges, lens, energy, labels, theta, tensors, w2, benv, right, ops)


def on_device(
    theta,
    boundary_env,
    right_env,
    site_tensors,
    site_mpo,
    bond_ops,
    block_energy,
    sector_charge,
    block_len,
    channel_charge,
):
    w2 = jnp.transpose(site_mpo[0], (0, 3, 2, 4, 1))
    w2 = jnp.pad(w2, ((0, 0), (0, 0), (0, 0), (0, 0), (0, WP - WCH)))
    w2 = w2.reshape(2, PH * WCH, PH * WP)
    w2 = jnp.pad(w2, ((0, 0), (0, 80 - PH * WCH), (0, BS - PH * WP)))
    lanczos, coef, env_out = sweep(
        channel_charge,
        block_len,
        block_energy,
        sector_charge,
        theta[0],
        site_tensors[0],
        w2,
        boundary_env,
        right_env[0],
        bond_ops[0],
    )
    return env_out[None], lanczos[None], coef


def solution(mesh):
    return jax.shard_map(
        on_device,
        mesh=mesh,
        in_specs=(
            P("site", ("blk", "charge"), None, None),
            P(("blk", "charge"), None, None, None),
            P("site", ("blk", "charge"), None, None, None),
            P("site", None, ("blk", "charge"), None, None, None),
            P("site", None, None, None, None, None),
            P("site", None, None, None),
            P("site", ("blk", "charge")),
            P("site", ("blk", "charge")),
            P("site", ("blk", "charge")),
            P(),
        ),
        out_specs=(
            P("site", ("blk", "charge"), None, None, None),
            P("site", ("blk", "charge"), None, None),
            P("site", None),
        ),
        check_vma=False,
    )
```

```python
import jax
import jax.numpy as jnp
from jax import lax
from jax.experimental import pallas as pl
from jax.experimental.pallas import tpu as pltpu
from jax.sharding import PartitionSpec as P

BS = 128
PH = 4
WCH = 18
WP = 24
MS = 73
CH = 128
GRP = 6
PRE = 0
PP = 16
M = 2048
NS = 64
SEC = 4
NBLK = 16
NDEV = 32
SIDE = 4
STEPS = (
    (1, 1), (3, 3), (2, 2), (1, 3), (3, 1), (2, 0), (0, 2), (1, 2),
    (3, 2), (2, 1), (2, 3), (1, 0), (3, 0), (0, 1), (0, 3),
)
F32 = jnp.float32
BF16 = jnp.bfloat16
MESH = pl.DeviceIdType.MESH
VMEM_LIMIT = 64 * 1024 * 1024 - 2400 * 1024


def mm(a, b):
    return jnp.dot(a, b, preferred_element_type=F32)


def loop(low, high, body):
    def step(i, carry):
        body(i)
        return carry

    lax.fori_loop(low, high, step, 0)


def env_site(a_ref, w_ref, l_ref, m_ref, at_ref, out_ref):
    for t in range(PH):
        at_ref[:, t * BS : (t + 1) * BS] = a_ref[t].T
    a_cat = jnp.concatenate([a_ref[s] for s in range(PH)], axis=1)
    w2 = w_ref[:, : PH * WP]

    def chunk(ci):
        base = pl.multiple_of(ci * (CH * WP), CH * WP)
        left = mm(l_ref[pl.ds(base, CH * WP), :].astype(BF16), a_cat)
        for j in range(0, CH, 2):
            sides = []
            for e in (j, j + 1):
                rows = left[e * WP : (e + 1) * WP]
                sides.append(
                    jnp.concatenate([rows[:, s * BS : (s + 1) * BS] for s in range(PH)], axis=0)
                )
            mixed = mm(w2, jnp.concatenate(sides, axis=1).astype(BF16))
            for e in range(2):
                m_ref[pl.ds((ci * CH + j + e) * MS, PH * WCH), :] = mixed[
                    : PH * WCH, e * BS : (e + 1) * BS
                ]

    loop(0, BS // CH, chunk)

    for v in range(0, WCH, 2):
        sides = []
        for e in range(2):
            sides.append(
                jnp.concatenate(
                    [m_ref[pl.ds(t * WCH + v + e, BS, stride=MS), :] for t in range(PH)], axis=0
                )
            )
        new = mm(at_ref[...], jnp.concatenate(sides, axis=1).astype(BF16))
        for e in range(2):
            one = new[:, e * BS : (e + 1) * BS]
            out_ref[v + e] = one.astype(BF16)
            l_ref[pl.ds(v + e, BS, stride=WP), :] = one


def build_kron(ops_ref, kron):
    big = (PP * PP, PP)
    rep = (
        lax.div(lax.broadcasted_iota(jnp.int32, big, 0), PP)
        == lax.broadcasted_iota(jnp.int32, big, 1)
    ).astype(F32).astype(BF16)
    wide = (PP, PP * PP)
    rep_t = (
        lax.div(lax.broadcasted_iota(jnp.int32, wide, 1), PP)
        == lax.broadcasted_iota(jnp.int32, wide, 0)
    ).astype(F32).astype(BF16)
    full = (PP * PP, PP * PP)
    same = lax.rem(lax.broadcasted_iota(jnp.int32, full, 0), PP) == lax.rem(
        lax.broadcasted_iota(jnp.int32, full, 1), PP
    )

    def one(w):
        rows = lax.dot_general(
            rep, ops_ref[w], (((1,), (1,)), ((), ())), preferred_element_type=F32
        ).astype(BF16)
        kron[w] = jnp.where(same, mm(rows, rep_t), 0.0).astype(BF16)

    loop(0, WCH, one)


def block_product(charge_ref, kron, tiles, env_ref, right_ref, mixed, states, acc):
    def group(wi):
        for e in range(GRP):
            w = wi * GRP + e
            charge = charge_ref[w]
            c = jnp.where(charge == 0, 2, jnp.where(charge < 0, 0, 1))
            big = kron[w]
            for g in range(4):
                sides = []
                for h in range(2):
                    r0 = (g * 2 + h) * 16
                    sides.append(tiles[:, c, r0 : r0 + 16, :].reshape(PP * 16, BS))
                part = mm(big, jnp.concatenate(sides, axis=1)).astype(BF16)
                for h in range(2):
                    r0 = (g * 2 + h) * 16
                    mixed[e, :, r0 : r0 + 16, :] = part[:, h * BS : (h + 1) * BS].reshape(
                        PP, 16, BS
                    )
        for e in range(GRP):
            env = env_ref[wi * GRP + e]
            for t in range(0, PP, 2):
                part = mm(env, jnp.concatenate([mixed[e, t], mixed[e, t + 1]], axis=1))
                part = part.astype(BF16)
                states[e, t] = part[:, :BS]
                states[e, t + 1] = part[:, BS:]
        right = right_ref[pl.ds(wi * GRP, GRP)].reshape(GRP * BS, BS)
        for t in range(0, PP, 4):
            both = jnp.concatenate(
                [states[e, t : t + 4].reshape(4 * BS, BS) for e in range(GRP)], axis=1
            )
            acc[t : t + 4] += mm(both, right).reshape(4, BS, BS)

    acc[...] = jnp.zeros_like(acc)
    loop(0, WCH // GRP, group)


def sweep_kernel(
    charge_ref,
    len_ref,
    energy_ref,
    label_ref,
    theta_ref,
    tens_ref,
    w2_ref,
    benv_ref,
    right_ref,
    ops_ref,
    lanczos_ref,
    coef_ref,
    envout_ref,
    tiles_a,
    tiles_b,
    recv1,
    send2,
    lab_mine,
    lab_all,
    table,
    table_s,
    tens,
    w2,
    left,
    mixer,
    at,
    envs,
    benv,
    right,
    ops,
    kron,
    mixed,
    states,
    acc,
    mine,
    stats,
    lab_send,
    lab_recv,
    one_send,
    one_recv,
    two_send,
    two_recv,
    ten_send,
    ten_recv,
    w_send,
    w_recv,
    env_send,
    env_recv,
    stat_send,
    stat_recv,
    local,
    tile_sem,
):
    z = lax.axis_index("site")
    blk = lax.axis_index("blk")
    core = lax.axis_index("charge")
    me = blk * 2 + core
    first = lax.div(z, 3)
    other = 1 - first
    tiles = (tiles_a, tiles_b)
    order = (first, other)

    def ahead(dx, dy):
        return lax.rem(lax.div(blk, SIDE) + dx, SIDE) * SIDE + lax.rem(lax.rem(blk, SIDE) + dy, SIDE)

    def arrived(ref, sem):
        pltpu.make_async_copy(ref, ref, sem).wait()

    def plane(off):
        dev = lax.rem(me + off, NDEV)
        return {"blk": lax.div(dev, 2), "charge": lax.rem(dev, 2)}

    barrier = pltpu.get_barrier_semaphore()
    loop(
        1,
        NDEV,
        lambda off: pl.semaphore_signal(
            barrier, inc=1, device_id=plane(off), device_id_type=MESH
        ),
    )
    for off in range(1, SEC):
        pl.semaphore_signal(
            barrier, inc=1, device_id={"site": lax.rem(z + off, SEC)}, device_id_type=MESH
        )

    def tile_load(turn, s):
        return pltpu.make_async_copy(
            theta_ref.at[order[turn], :, pl.ds(pl.multiple_of(s * BS, BS), BS)],
            tiles[turn].at[s, 2],
            tile_sem.at[turn],
        )

    for turn in range(2):
        loop(0, PP, lambda s: tile_load(turn, s).start())
    loads = [
        pltpu.make_async_copy(benv_ref, benv, local.at[0]),
        pltpu.make_async_copy(tens_ref, tens.at[z], local.at[1]),
        pltpu.make_async_copy(w2_ref, w2.at[z, 0], local.at[2]),
        pltpu.make_async_copy(w2_ref, w2.at[z, 1], local.at[3]),
        pltpu.make_async_copy(right_ref, right, local.at[4]),
        pltpu.make_async_copy(ops_ref, ops, local.at[6]),
    ]
    for copy in loads:
        copy.start()

    lane = lax.broadcasted_iota(jnp.int32, (8, BS), 1)
    line = lax.broadcasted_iota(jnp.int32, (8, BS), 0)
    row = jnp.zeros((8, BS), jnp.int32)
    for k in range(2):
        here = (line == core) & (lane == label_ref[0, k] + 1)
        row = row + jnp.where(here, 2 * blk + k + 1, 0)
        row = row + jnp.where((line == 2) & (lane == 2 * me + k), label_ref[0, k], 0)
    lab_mine[...] = row
    lab_all[me] = row
    recv1[0] = jnp.zeros((BS, BS), BF16)
    rows = lax.broadcasted_iota(jnp.int32, (BS, BS), 0)

    def mask(s):
        for turn in range(2):
            tile = tiles[turn][s, 2].astype(F32)
            tiles[turn][s, 2] = jnp.where(rows < len_ref[0, order[turn]], tile, 0.0).astype(BF16)

    for turn in range(2):
        arrived(tiles[turn].at[:, 2], tile_sem.at[turn])
    loop(0, PP, mask)
    for turn in range(2):
        recv1[1 + 2 * blk + order[turn]] = tiles[turn][blk, 2]
    pl.semaphore_wait(barrier, NDEV - 1 + SEC - 1)

    def labels_to(off):
        return pltpu.make_async_remote_copy(
            src_ref=lab_mine,
            dst_ref=lab_all.at[me],
            send_sem=lab_send,
            recv_sem=lab_recv,
            device_id=plane(off),
            device_id_type=MESH,
        )

    def piece_to(turn, dev):
        return pltpu.make_async_remote_copy(
            src_ref=tiles[turn].at[dev, 2],
            dst_ref=recv1.at[1 + 2 * blk + order[turn]],
            send_sem=one_send,
            recv_sem=one_recv,
            device_id={"blk": dev},
            device_id_type=MESH,
        )

    def picked_to(turn, dev):
        return pltpu.make_async_remote_copy(
            src_ref=send2.at[turn, dev],
            dst_ref=tiles[turn].at[blk, pl.ds(0, 2)],
            send_sem=two_send.at[turn],
            recv_sem=two_recv.at[turn],
            device_id={"blk": dev, "charge": 1 - core},
            device_id_type=MESH,
        )

    def tensors_to(dst, k, sec):
        return pltpu.make_async_remote_copy(
            src_ref=tens_ref.at[:, k],
            dst_ref=tens.at[z, :, k],
            send_sem=ten_send.at[dst, k],
            recv_sem=ten_recv.at[sec, k],
            device_id={"site": dst},
            device_id_type=MESH,
        )

    def mixer_to(dst, k, sec):
        return pltpu.make_async_remote_copy(
            src_ref=w2_ref,
            dst_ref=w2.at[z, k],
            send_sem=w_send.at[dst, k],
            recv_sem=w_recv.at[sec, k],
            device_id={"site": dst},
            device_id_type=MESH,
        )

    routes = (
        (0, 3, 1), (0, 2, 0), (0, 1, 0), (0, 1, 1),
        (1, 3, 1), (1, 2, 0), (2, 3, 1),
    )

    loop(1, NDEV, lambda off: labels_to(off).start())
    for src, dst, k in routes:

        @pl.when(z == src)
        def _():
            mixer_to(dst, k, src).start()
            tensors_to(dst, k, src).start()

    for turn in range(2):
        for dx, dy in STEPS:
            piece_to(turn, ahead(dx, dy)).start()

    for copy in loads:
        copy.wait()
    build_kron(ops, kron)

    def load_left(k, env_ref):
        left[k] = jnp.zeros((BS * WP, BS), F32)

        def one(v):
            left[k, pl.ds(v, BS, stride=WP), :] = env_ref[v].astype(F32)

        loop(0, WCH, one)

    for k in range(2):

        @pl.when((z < 2) | (z == k + 2))
        def _():
            load_left(k, benv.at[k])

        @pl.when(z == 0)
        def _():
            envs[0, k] = benv[k]

    def send_picked():
        arrived(lab_all.at[pl.ds(0, NDEV - 1)], lab_recv)
        total = jnp.zeros((8, BS), jnp.int32)
        for i in range(NDEV):
            total = total + lab_all[i]
        table[...] = total
        to_scalar = pltpu.make_async_copy(table, table_s, local.at[5])
        to_scalar.start()
        to_scalar.wait()
        arrived(recv1.at[pl.ds(0, 2 * NBLK - 2)], one_recv)
        for turn in range(2):

            def pick(dev):
                label = table_s[2, 4 * dev + 2 * (1 - core) + order[turn]]
                for gi in range(2):
                    send2[turn, dev, gi] = recv1[table_s[core, label + 2 * gi]]

            loop(0, NBLK, pick)
            for dx, dy in STEPS + ((0, 0),):
                picked_to(turn, ahead(dx, dy)).start()

    def env_to(slot, k, dst):
        return pltpu.make_async_remote_copy(
            src_ref=envs.at[slot, k],
            dst_ref=envs.at[0, k],
            send_sem=env_send,
            recv_sem=env_recv,
            device_id={"site": dst},
            device_id_type=MESH,
        )

    env_routes = ((2, 5, 1, 0, 3), (3, 3, 2, 1, 2))

    def site(q):
        unit, i = lax.div(q, 2), lax.rem(q, 2)
        sec = jnp.where(z < 2, lax.div(unit, 2), unit)
        k = jnp.where(z < 2, lax.rem(unit, 2), z - 2)

        @pl.when(q == PRE)
        def _():
            send_picked()

        @pl.when((i == 0) & (sec != z))
        def _():
            mixer_to(0, k, sec).wait_recv()
            tensors_to(0, k, sec).wait_recv()

        slot = jnp.where(sec == z, 1, 0)
        slot = jnp.where((z == 3) & (sec == 1), 2, slot)
        env_site(tens.at[sec, i, k], w2.at[sec, k, i], left.at[k], mixer, at, envs.at[slot, k])
        for src, when, slot_at, kk, dst in env_routes:

            @pl.when((z == src) & (q == when))
            def _():
                env_to(slot_at, kk, dst).start()

    loop(0, jnp.where(z == 0, 4, jnp.where(z == 2, 6, 8)), site)

    def late_sites():
        env_to(0, 0, 0).wait_recv()
        load_left(other, envs.at[0, other])

        def late(i):
            env_site(
                tens.at[z, i, other], w2.at[z, other, i], left.at[other], mixer, at, envs.at[1, other]
            )

        loop(0, 2, late)

    zero = jnp.zeros((8, BS), F32)

    def fold(x):
        return jnp.sum(x.reshape(16, 8, BS), axis=0)

    def everywhere(x):
        return jnp.broadcast_to(
            jnp.sum(jnp.sum(x, axis=0, keepdims=True), axis=1, keepdims=True), (1, BS)
        )

    def block_sums(turn):
        length, energy = len_ref[0, order[turn]], energy_ref[0, order[turn]]

        def sums_one(t, carry):
            cor, nor = carry
            th = tiles[turn][t, 2].astype(F32)
            p = jnp.where(rows < length, acc[turn, t], 0.0) - energy * th
            acc[turn, t] = p
            return cor + fold(p * th), nor + fold(th * th)

        cor, nor = lax.fori_loop(0, PP, sums_one, (zero, zero))
        cor, nor = everywhere(cor), everywhere(nor)
        rho = jnp.where(nor > 0, cor / jnp.where(nor > 0, nor, 1.0), 0.0)

        def sums_two(t, carry):
            sq, cross = carry
            th = tiles[turn][t, 2].astype(F32)
            r = acc[turn, t] - rho * th
            return sq + fold(r * r), cross + fold(r * th)

        sq, cross = lax.fori_loop(0, PP, sums_two, (zero, zero))
        mine[8 * turn : 8 * turn + 8] = jnp.concatenate(
            [cor, nor, everywhere(sq), everywhere(cross), rho, jnp.zeros((3, BS), F32)], axis=0
        )

    for turn in range(2):
        k = order[turn]
        if turn:
            pl.when(z >= 2)(late_sites)
            env_store = pltpu.make_async_copy(envs.at[1], envout_ref, local.at[7])
            env_store.start()
        arrived(tiles[turn].at[:, pl.ds(0, 2)], two_recv.at[turn])
        block_product(
            charge_ref, kron, tiles[turn], envs.at[0, k], right.at[k], mixed, states, acc.at[turn]
        )
        block_sums(turn)


    stats[me] = mine[...]

    def stat_to(off):
        return pltpu.make_async_remote_copy(
            src_ref=mine,
            dst_ref=stats.at[me],
            send_sem=stat_send,
            recv_sem=stat_recv,
            device_id=plane(off),
            device_id_type=MESH,
        )

    loop(1, NDEV, lambda off: stat_to(off).start())
    arrived(lab_all.at[pl.ds(0, NDEV - 1)], lab_send)
    arrived(recv1.at[pl.ds(0, 2 * NBLK - 2)], one_send)
    for turn in range(2):
        arrived(send2.at[turn], two_send.at[turn])
    for src, dst, k in routes:

        @pl.when(z == src)
        def _():
            mixer_to(dst, k, src).wait_send()
            tensors_to(dst, k, src).wait_send()

    for src, when, slot_at, kk, dst in env_routes:

        @pl.when(z == src)
        def _():
            env_to(slot_at, kk, dst).wait_send()

    arrived(stats.at[pl.ds(0, NDEV - 1)], stat_recv)

    cor_all = jnp.zeros((1, BS), F32)
    nor_all = jnp.zeros((1, BS), F32)
    for i in range(NDEV):
        for at_row in (0, 8):
            cor_all = cor_all + stats[i, at_row : at_row + 1]
            nor_all = nor_all + stats[i, at_row + 1 : at_row + 2]
    ray = cor_all / nor_all
    res = jnp.zeros((1, BS), F32)
    for i in range(NDEV):
        for at_row in (0, 8):
            nor, sq, cross, rho = (
                stats[i, at_row + j : at_row + j + 1] for j in (1, 2, 3, 4)
            )
            gap = rho - ray
            res = res + (sq + gap * (2.0 * cross + gap * nor))
    mean_sq = jnp.maximum(res, 0.0) / (NS * BS * M)
    scale = 1.0 / jnp.sqrt(mean_sq + 1e-06)

    def finish(t):
        for turn in range(2):
            th = tiles[turn][t, 2].astype(F32)
            lanczos_ref[order[turn], :, pl.ds(pl.multiple_of(t * BS, BS), BS)] = (
                (acc[turn, t] - ray * th) * scale
            ).astype(BF16)

    loop(0, PP, finish)
    coef_ref[0, 0] = ray[0, 0]
    coef_ref[0, 1] = jnp.sqrt(mean_sq)[0, 0]
    arrived(stats.at[pl.ds(0, NDEV - 1)], stat_send)
    env_store.wait()


def sweep(charges, lens, energy, labels, theta, tensors, w2, benv, right, ops):
    hbm = pl.BlockSpec(memory_space=pltpu.HBM)
    vmem = pl.BlockSpec(memory_space=pltpu.VMEM)
    smem = pl.BlockSpec(memory_space=pltpu.SMEM)
    dma = pltpu.SemaphoreType.DMA
    return pl.pallas_call(
        sweep_kernel,
        out_shape=(
            pltpu.VMEM((2, BS, M), BF16),
            jax.ShapeDtypeStruct((1, 2), F32),
            pltpu.VMEM((2, WCH, BS, BS), BF16),
        ),
        in_specs=[smem] * 4 + [hbm] * 6,
        out_specs=(vmem, smem, vmem),
        scratch_shapes=[
            pltpu.VMEM((PP, 3, BS, BS), BF16),
            pltpu.VMEM((PP, 3, BS, BS), BF16),
            pltpu.VMEM((NDEV + 1, BS, BS), BF16),
            pltpu.VMEM((2, NBLK, 2, BS, BS), BF16),
            pltpu.VMEM((8, BS), jnp.int32),
            pltpu.VMEM((NDEV, 8, BS), jnp.int32),
            pltpu.VMEM((8, BS), jnp.int32),
            pltpu.SMEM((8, BS), jnp.int32),
            pltpu.VMEM((SEC, 2, 2, PH, BS, BS), BF16),
            pltpu.VMEM((SEC, 2, 2, 80, BS), BF16),
            pltpu.VMEM((2, BS * WP, BS), F32),
            pltpu.VMEM((BS * MS, BS), F32),
            pltpu.VMEM((BS, PH * BS), BF16),
            pltpu.VMEM((3, 2, WCH, BS, BS), BF16),
            pltpu.VMEM((2, WCH, BS, BS), BF16),
            pltpu.VMEM((2, WCH, BS, BS), BF16),
            pltpu.VMEM((WCH, PP, PP), BF16),
            pltpu.VMEM((WCH, PP * PP, PP * PP), BF16),
            pltpu.VMEM((GRP, PP, BS, BS), BF16),
            pltpu.VMEM((GRP, PP, BS, BS), BF16),
            pltpu.VMEM((2, PP, BS, BS), F32),
            pltpu.VMEM((16, BS), F32),
            pltpu.VMEM((NDEV, 16, BS), F32),
            dma,
            dma,
            dma,
            dma,
            dma((2,)),
            dma((2,)),
            dma((SEC, 2)),
            dma((SEC, 2)),
            dma((SEC, 2)),
            dma((SEC, 2)),
            dma,
            dma,
            dma,
            dma,
            dma((8,)),
            dma((2,)),
        ],
        compiler_params=pltpu.CompilerParams(
            collective_id=0, has_side_effects=True, vmem_limit_bytes=VMEM_LIMIT
        ),
        name="sweep",
    )(charges, lens, energy, labels, theta, tensors, w2, benv, right, ops)


def on_device(
    theta,
    boundary_env,
    right_env,
    site_tensors,
    site_mpo,
    bond_ops,
    block_energy,
    sector_charge,
    block_len,
    channel_charge,
):
    w2 = jnp.transpose(site_mpo[0], (0, 3, 2, 4, 1))
    w2 = jnp.pad(w2, ((0, 0), (0, 0), (0, 0), (0, 0), (0, WP - WCH)))
    w2 = w2.reshape(2, PH * WCH, PH * WP)
    w2 = jnp.pad(w2, ((0, 0), (0, 80 - PH * WCH), (0, BS - PH * WP)))
    lanczos, coef, env_out = sweep(
        channel_charge,
        block_len,
        block_energy,
        sector_charge,
        theta[0],
        site_tensors[0],
        w2,
        boundary_env,
        right_env[0],
        bond_ops[0],
    )
    return env_out[None], lanczos[None], coef


def solution(mesh):
    return jax.shard_map(
        on_device,
        mesh=mesh,
        in_specs=(
            P("site", ("blk", "charge"), None, None),
            P(("blk", "charge"), None, None, None),
            P("site", ("blk", "charge"), None, None, None),
            P("site", None, ("blk", "charge"), None, None, None),
            P("site", None, None, None, None, None),
            P("site", None, None, None),
            P("site", ("blk", "charge")),
            P("site", ("blk", "charge")),
            P("site", ("blk", "charge")),
            P(),
        ),
        out_specs=(
            P("site", ("blk", "charge"), None, None, None),
            P("site", ("blk", "charge"), None, None),
            P("site", None),
        ),
        check_vma=False,
    )
```

```python
import jax
import jax.numpy as jnp
from jax import lax
from jax.experimental import pallas as pl
from jax.experimental.pallas import tpu as pltpu
from jax.sharding import PartitionSpec as P

BS = 128
PH = 4
WCH = 18
WP = 24
MS = 73
CH = 128
GRP = 6
PRE = 0
PP = 16
M = 2048
NS = 64
SEC = 4
NBLK = 16
NDEV = 32
SIDE = 4
STEPS = (
    (1, 1), (3, 3), (2, 2), (1, 3), (3, 1), (2, 0), (0, 2), (1, 2),
    (3, 2), (2, 1), (2, 3), (1, 0), (3, 0), (0, 1), (0, 3),
)
F32 = jnp.float32
BF16 = jnp.bfloat16
MESH = pl.DeviceIdType.MESH
VMEM_LIMIT = 64 * 1024 * 1024 - 2400 * 1024


def mm(a, b):
    return jnp.dot(a, b, preferred_element_type=F32)


def loop(low, high, body):
    def step(i, carry):
        body(i)
        return carry

    lax.fori_loop(low, high, step, 0)


def env_site(a_ref, w_ref, l_ref, m_ref, at_ref, out_ref):
    for t in range(PH):
        at_ref[:, t * BS : (t + 1) * BS] = a_ref[t].T
    a_cat = jnp.concatenate([a_ref[s] for s in range(PH)], axis=1)
    w2 = w_ref[:, : PH * WP]

    def chunk(ci):
        base = pl.multiple_of(ci * (CH * WP), CH * WP)
        left = mm(l_ref[pl.ds(base, CH * WP), :].astype(BF16), a_cat)
        for j in range(0, CH, 2):
            sides = []
            for e in (j, j + 1):
                rows = left[e * WP : (e + 1) * WP]
                sides.append(
                    jnp.concatenate([rows[:, s * BS : (s + 1) * BS] for s in range(PH)], axis=0)
                )
            mixed = mm(w2, jnp.concatenate(sides, axis=1).astype(BF16))
            for e in range(2):
                m_ref[pl.ds((ci * CH + j + e) * MS, PH * WCH), :] = mixed[
                    : PH * WCH, e * BS : (e + 1) * BS
                ]

    loop(0, BS // CH, chunk)

    for v in range(0, WCH, 2):
        sides = []
        for e in range(2):
            sides.append(
                jnp.concatenate(
                    [m_ref[pl.ds(t * WCH + v + e, BS, stride=MS), :] for t in range(PH)], axis=0
                )
            )
        new = mm(at_ref[...], jnp.concatenate(sides, axis=1).astype(BF16))
        for e in range(2):
            one = new[:, e * BS : (e + 1) * BS]
            out_ref[v + e] = one.astype(BF16)
            l_ref[pl.ds(v + e, BS, stride=WP), :] = one


def iota(shape, dim):
    return lax.broadcasted_iota(jnp.int32, shape, dim)


def ones_where(condition):
    return jnp.where(condition, 1.0, 0.0).astype(BF16)


def first_dims(a, b):
    return lax.dot_general(a, b, (((0,), (0,)), ((), ())), preferred_element_type=F32)


def build_mixer(mpo_ref, mixer_ref):
    tall = (WCH * PP, BS)
    row, lane = iota(tall, 0), iota(tall, 1)
    wanted = lax.rem(row, PH) * WP + lax.div(row, PP)
    place = (80, WCH)
    for i in range(2):
        total = jnp.zeros((80, BS), F32)
        for t in range(PH):
            pick = ones_where((lax.rem(lax.div(row, PH), PH) == t) & (lane == wanted))
            part = first_dims(mpo_ref[i], pick).astype(BF16)
            put = ones_where(iota(place, 0) == t * WCH + iota(place, 1))
            total = total + mm(put, part)
        mixer_ref[i] = total.astype(BF16)


def build_kron(ops_ref, lines, kron):
    full = (PP * PP, PP * PP)
    row, lane = iota(full, 0), iota(full, 1)
    lines[...] = first_dims(ops_ref[...], ones_where(row == lane))
    spread = ones_where(lax.div(row, PP) == lax.div(lane, PP))

    def one(w):
        value = jnp.broadcast_to(lines[pl.ds(w, 1), :], full)
        here = jnp.where(lax.div(row, PP) == lax.rem(lane, PP), value, 0.0).astype(BF16)
        same = lax.rem(row, PP) == lax.rem(lane, PP)
        kron[w] = jnp.where(same, mm(here, spread), 0.0).astype(BF16)

    loop(0, WCH, one)


def block_product(charge_ref, kron, tiles, env_ref, right_ref, mixed, states, acc):
    def group(wi):
        for e in range(GRP):
            w = wi * GRP + e
            charge = charge_ref[w]
            c = jnp.where(charge == 0, 2, jnp.where(charge < 0, 0, 1))
            big = kron[w]
            for g in range(4):
                sides = []
                for h in range(2):
                    r0 = (g * 2 + h) * 16
                    sides.append(tiles[:, c, r0 : r0 + 16, :].reshape(PP * 16, BS))
                part = mm(big, jnp.concatenate(sides, axis=1)).astype(BF16)
                for h in range(2):
                    r0 = (g * 2 + h) * 16
                    mixed[e, :, r0 : r0 + 16, :] = part[:, h * BS : (h + 1) * BS].reshape(
                        PP, 16, BS
                    )
        for e in range(GRP):
            env = env_ref[wi * GRP + e]
            for t in range(0, PP, 2):
                part = mm(env, jnp.concatenate([mixed[e, t], mixed[e, t + 1]], axis=1))
                part = part.astype(BF16)
                states[e, t] = part[:, :BS]
                states[e, t + 1] = part[:, BS:]
        right = right_ref[pl.ds(wi * GRP, GRP)].reshape(GRP * BS, BS)
        for t in range(0, PP, 4):
            both = jnp.concatenate(
                [states[e, t : t + 4].reshape(4 * BS, BS) for e in range(GRP)], axis=1
            )
            acc[t : t + 4] += mm(both, right).reshape(4, BS, BS)

    acc[...] = jnp.zeros_like(acc)
    loop(0, WCH // GRP, group)


def sweep_kernel(
    charge_ref,
    len_ref,
    energy_ref,
    label_ref,
    theta_ref,
    tens_ref,
    mpo_ref,
    benv_ref,
    right_ref,
    ops_ref,
    lanczos_ref,
    coef_ref,
    envout_ref,
    tiles_a,
    tiles_b,
    recv1,
    send2,
    lab_mine,
    lab_all,
    table,
    table_s,
    tens,
    w2,
    left,
    mixer,
    at,
    envs,
    benv,
    right,
    ops,
    lines,
    w2_ref,
    mpo,
    kron,
    mixed,
    states,
    acc,
    mine,
    stats,
    lab_send,
    lab_recv,
    one_send,
    one_recv,
    two_send,
    two_recv,
    ten_send,
    ten_recv,
    w_send,
    w_recv,
    env_send,
    env_recv,
    stat_send,
    stat_recv,
    local,
    tile_sem,
):
    z = lax.axis_index("site")
    blk = lax.axis_index("blk")
    core = lax.axis_index("charge")
    me = blk * 2 + core
    first = lax.div(z, 3)
    other = 1 - first
    tiles = (tiles_a, tiles_b)
    order = (first, other)

    def ahead(dx, dy):
        return lax.rem(lax.div(blk, SIDE) + dx, SIDE) * SIDE + lax.rem(lax.rem(blk, SIDE) + dy, SIDE)

    def arrived(ref, sem):
        pltpu.make_async_copy(ref, ref, sem).wait()

    def plane(off):
        dev = lax.rem(me + off, NDEV)
        return {"blk": lax.div(dev, 2), "charge": lax.rem(dev, 2)}

    barrier = pltpu.get_barrier_semaphore()
    loop(
        1,
        NDEV,
        lambda off: pl.semaphore_signal(
            barrier, inc=1, device_id=plane(off), device_id_type=MESH
        ),
    )
    for off in range(1, SEC):
        pl.semaphore_signal(
            barrier, inc=1, device_id={"site": lax.rem(z + off, SEC)}, device_id_type=MESH
        )

    def tile_load(turn, s):
        return pltpu.make_async_copy(
            theta_ref.at[order[turn], :, pl.ds(pl.multiple_of(s * BS, BS), BS)],
            tiles[turn].at[s, 2],
            tile_sem.at[turn],
        )

    for turn in range(2):
        loop(0, PP, lambda s: tile_load(turn, s).start())
    loads = [
        pltpu.make_async_copy(benv_ref, benv, local.at[0]),
        pltpu.make_async_copy(tens_ref, tens.at[z], local.at[1]),
        pltpu.make_async_copy(right_ref, right, local.at[4]),
        pltpu.make_async_copy(ops_ref, ops, local.at[6]),
    ]
    load_mpo = pltpu.make_async_copy(mpo_ref, mpo, local.at[2])
    load_mpo.start()
    for copy in loads:
        copy.start()

    lane = lax.broadcasted_iota(jnp.int32, (8, BS), 1)
    line = lax.broadcasted_iota(jnp.int32, (8, BS), 0)
    row = jnp.zeros((8, BS), jnp.int32)
    for k in range(2):
        here = (line == core) & (lane == label_ref[0, k] + 1)
        row = row + jnp.where(here, 2 * blk + k + 1, 0)
        row = row + jnp.where((line == 2) & (lane == 2 * me + k), label_ref[0, k], 0)
    lab_mine[...] = row
    lab_all[me] = row
    recv1[0] = jnp.zeros((BS, BS), BF16)
    rows = lax.broadcasted_iota(jnp.int32, (BS, BS), 0)

    def mask(s):
        for turn in range(2):
            tile = tiles[turn][s, 2].astype(F32)
            tiles[turn][s, 2] = jnp.where(rows < len_ref[0, order[turn]], tile, 0.0).astype(BF16)

    for turn in range(2):
        arrived(tiles[turn].at[:, 2], tile_sem.at[turn])
    loop(0, PP, mask)
    load_mpo.wait()
    build_mixer(mpo, w2_ref)
    for k in range(2):
        w2[z, k] = w2_ref[...]
    for turn in range(2):
        recv1[1 + 2 * blk + order[turn]] = tiles[turn][blk, 2]
    pl.semaphore_wait(barrier, NDEV - 1 + SEC - 1)

    def labels_to(off):
        return pltpu.make_async_remote_copy(
            src_ref=lab_mine,
            dst_ref=lab_all.at[me],
            send_sem=lab_send,
            recv_sem=lab_recv,
            device_id=plane(off),
            device_id_type=MESH,
        )

    def piece_to(turn, dev):
        return pltpu.make_async_remote_copy(
            src_ref=tiles[turn].at[dev, 2],
            dst_ref=recv1.at[1 + 2 * blk + order[turn]],
            send_sem=one_send,
            recv_sem=one_recv,
            device_id={"blk": dev},
            device_id_type=MESH,
        )

    def picked_to(turn, dev):
        return pltpu.make_async_remote_copy(
            src_ref=send2.at[turn, dev],
            dst_ref=tiles[turn].at[blk, pl.ds(0, 2)],
            send_sem=two_send.at[turn],
            recv_sem=two_recv.at[turn],
            device_id={"blk": dev, "charge": 1 - core},
            device_id_type=MESH,
        )

    def tensors_to(dst, k, sec):
        return pltpu.make_async_remote_copy(
            src_ref=tens_ref.at[:, k],
            dst_ref=tens.at[z, :, k],
            send_sem=ten_send.at[dst, k],
            recv_sem=ten_recv.at[sec, k],
            device_id={"site": dst},
            device_id_type=MESH,
        )

    def mixer_to(dst, k, sec):
        return pltpu.make_async_remote_copy(
            src_ref=w2_ref,
            dst_ref=w2.at[z, k],
            send_sem=w_send.at[dst, k],
            recv_sem=w_recv.at[sec, k],
            device_id={"site": dst},
            device_id_type=MESH,
        )

    routes = (
        (0, 3, 1), (0, 2, 0), (0, 1, 0), (0, 1, 1),
        (1, 3, 1), (1, 2, 0), (2, 3, 1),
    )

    loop(1, NDEV, lambda off: labels_to(off).start())
    for src, dst, k in routes:

        @pl.when(z == src)
        def _():
            mixer_to(dst, k, src).start()
            tensors_to(dst, k, src).start()

    for turn in range(2):
        for dx, dy in STEPS:
            piece_to(turn, ahead(dx, dy)).start()

    for copy in loads:
        copy.wait()
    build_kron(ops, lines, kron)

    def load_left(k, env_ref):
        left[k] = jnp.zeros((BS * WP, BS), F32)

        def one(v):
            left[k, pl.ds(v, BS, stride=WP), :] = env_ref[v].astype(F32)

        loop(0, WCH, one)

    for k in range(2):

        @pl.when((z < 2) | (z == k + 2))
        def _():
            load_left(k, benv.at[k])

        @pl.when(z == 0)
        def _():
            envs[0, k] = benv[k]

    def send_picked():
        arrived(lab_all.at[pl.ds(0, NDEV - 1)], lab_recv)
        total = jnp.zeros((8, BS), jnp.int32)
        for i in range(NDEV):
            total = total + lab_all[i]
        table[...] = total
        to_scalar = pltpu.make_async_copy(table, table_s, local.at[5])
        to_scalar.start()
        to_scalar.wait()
        arrived(recv1.at[pl.ds(0, 2 * NBLK - 2)], one_recv)
        for turn in range(2):

            def pick(dev):
                label = table_s[2, 4 * dev + 2 * (1 - core) + order[turn]]
                for gi in range(2):
                    send2[turn, dev, gi] = recv1[table_s[core, label + 2 * gi]]

            loop(0, NBLK, pick)
            for dx, dy in STEPS + ((0, 0),):
                picked_to(turn, ahead(dx, dy)).start()

    def env_to(slot, k, dst):
        return pltpu.make_async_remote_copy(
            src_ref=envs.at[slot, k],
            dst_ref=envs.at[0, k],
            send_sem=env_send,
            recv_sem=env_recv,
            device_id={"site": dst},
            device_id_type=MESH,
        )

    env_routes = ((2, 5, 1, 0, 3), (3, 3, 2, 1, 2))

    def site(q):
        unit, i = lax.div(q, 2), lax.rem(q, 2)
        sec = jnp.where(z < 2, lax.div(unit, 2), unit)
        k = jnp.where(z < 2, lax.rem(unit, 2), z - 2)

        @pl.when(q == PRE)
        def _():
            send_picked()

        @pl.when((i == 0) & (sec != z))
        def _():
            mixer_to(0, k, sec).wait_recv()
            tensors_to(0, k, sec).wait_recv()

        slot = jnp.where(sec == z, 1, 0)
        slot = jnp.where((z == 3) & (sec == 1), 2, slot)
        env_site(tens.at[sec, i, k], w2.at[sec, k, i], left.at[k], mixer, at, envs.at[slot, k])
        for src, when, slot_at, kk, dst in env_routes:

            @pl.when((z == src) & (q == when))
            def _():
                env_to(slot_at, kk, dst).start()

    loop(0, jnp.where(z == 0, 4, jnp.where(z == 2, 6, 8)), site)

    def late_sites():
        env_to(0, 0, 0).wait_recv()
        load_left(other, envs.at[0, other])

        def late(i):
            env_site(
                tens.at[z, i, other], w2.at[z, other, i], left.at[other], mixer, at, envs.at[1, other]
            )

        loop(0, 2, late)

    zero = jnp.zeros((8, BS), F32)

    def fold(x):
        return jnp.sum(x.reshape(16, 8, BS), axis=0)

    def everywhere(x):
        return jnp.broadcast_to(
            jnp.sum(jnp.sum(x, axis=0, keepdims=True), axis=1, keepdims=True), (1, BS)
        )

    def block_sums(turn):
        length, energy = len_ref[0, order[turn]], energy_ref[0, order[turn]]

        def sums_one(t, carry):
            cor, nor = carry
            th = tiles[turn][t, 2].astype(F32)
            p = jnp.where(rows < length, acc[turn, t], 0.0) - energy * th
            acc[turn, t] = p
            return cor + fold(p * th), nor + fold(th * th)

        cor, nor = lax.fori_loop(0, PP, sums_one, (zero, zero))
        cor, nor = everywhere(cor), everywhere(nor)
        rho = jnp.where(nor > 0, cor / jnp.where(nor > 0, nor, 1.0), 0.0)

        def sums_two(t, carry):
            sq, cross = carry
            th = tiles[turn][t, 2].astype(F32)
            r = acc[turn, t] - rho * th
            return sq + fold(r * r), cross + fold(r * th)

        sq, cross = lax.fori_loop(0, PP, sums_two, (zero, zero))
        mine[8 * turn : 8 * turn + 8] = jnp.concatenate(
            [cor, nor, everywhere(sq), everywhere(cross), rho, jnp.zeros((3, BS), F32)], axis=0
        )

    for turn in range(2):
        k = order[turn]
        if turn:
            pl.when(z >= 2)(late_sites)
            env_store = pltpu.make_async_copy(envs.at[1], envout_ref, local.at[7])
            env_store.start()
        arrived(tiles[turn].at[:, pl.ds(0, 2)], two_recv.at[turn])
        block_product(
            charge_ref, kron, tiles[turn], envs.at[0, k], right.at[k], mixed, states, acc.at[turn]
        )
        block_sums(turn)


    stats[me] = mine[...]

    def stat_to(off):
        return pltpu.make_async_remote_copy(
            src_ref=mine,
            dst_ref=stats.at[me],
            send_sem=stat_send,
            recv_sem=stat_recv,
            device_id=plane(off),
            device_id_type=MESH,
        )

    loop(1, NDEV, lambda off: stat_to(off).start())
    arrived(lab_all.at[pl.ds(0, NDEV - 1)], lab_send)
    arrived(recv1.at[pl.ds(0, 2 * NBLK - 2)], one_send)
    for turn in range(2):
        arrived(send2.at[turn], two_send.at[turn])
    for src, dst, k in routes:

        @pl.when(z == src)
        def _():
            mixer_to(dst, k, src).wait_send()
            tensors_to(dst, k, src).wait_send()

    for src, when, slot_at, kk, dst in env_routes:

        @pl.when(z == src)
        def _():
            env_to(slot_at, kk, dst).wait_send()

    arrived(stats.at[pl.ds(0, NDEV - 1)], stat_recv)

    cor_all = jnp.zeros((1, BS), F32)
    nor_all = jnp.zeros((1, BS), F32)
    for i in range(NDEV):
        for at_row in (0, 8):
            cor_all = cor_all + stats[i, at_row : at_row + 1]
            nor_all = nor_all + stats[i, at_row + 1 : at_row + 2]
    ray = cor_all / nor_all
    res = jnp.zeros((1, BS), F32)
    for i in range(NDEV):
        for at_row in (0, 8):
            nor, sq, cross, rho = (
                stats[i, at_row + j : at_row + j + 1] for j in (1, 2, 3, 4)
            )
            gap = rho - ray
            res = res + (sq + gap * (2.0 * cross + gap * nor))
    mean_sq = jnp.maximum(res, 0.0) / (NS * BS * M)
    scale = 1.0 / jnp.sqrt(mean_sq + 1e-06)

    def finish(t):
        for turn in range(2):
            th = tiles[turn][t, 2].astype(F32)
            lanczos_ref[order[turn], :, pl.ds(pl.multiple_of(t * BS, BS), BS)] = (
                (acc[turn, t] - ray * th) * scale
            ).astype(BF16)

    loop(0, PP, finish)
    coef_ref[0, 0] = ray[0, 0]
    coef_ref[0, 1] = jnp.sqrt(mean_sq)[0, 0]
    arrived(stats.at[pl.ds(0, NDEV - 1)], stat_send)
    env_store.wait()


def sweep(charges, lens, energy, labels, theta, tensors, mpo, benv, right, ops):
    hbm = pl.BlockSpec(memory_space=pltpu.HBM)
    vmem = pl.BlockSpec(memory_space=pltpu.VMEM)
    smem = pl.BlockSpec(memory_space=pltpu.SMEM)
    dma = pltpu.SemaphoreType.DMA
    return pl.pallas_call(
        sweep_kernel,
        out_shape=(
            pltpu.VMEM((2, BS, M), BF16),
            jax.ShapeDtypeStruct((1, 2), F32),
            pltpu.VMEM((2, WCH, BS, BS), BF16),
        ),
        in_specs=[smem] * 4 + [hbm] * 6,
        out_specs=(vmem, smem, vmem),
        scratch_shapes=[
            pltpu.VMEM((PP, 3, BS, BS), BF16),
            pltpu.VMEM((PP, 3, BS, BS), BF16),
            pltpu.VMEM((NDEV + 1, BS, BS), BF16),
            pltpu.VMEM((2, NBLK, 2, BS, BS), BF16),
            pltpu.VMEM((8, BS), jnp.int32),
            pltpu.VMEM((NDEV, 8, BS), jnp.int32),
            pltpu.VMEM((8, BS), jnp.int32),
            pltpu.SMEM((8, BS), jnp.int32),
            pltpu.VMEM((SEC, 2, 2, PH, BS, BS), BF16),
            pltpu.VMEM((SEC, 2, 2, 80, BS), BF16),
            pltpu.VMEM((2, BS * WP, BS), F32),
            pltpu.VMEM((BS * MS, BS), F32),
            pltpu.VMEM((BS, PH * BS), BF16),
            pltpu.VMEM((3, 2, WCH, BS, BS), BF16),
            pltpu.VMEM((2, WCH, BS, BS), BF16),
            pltpu.VMEM((2, WCH, BS, BS), BF16),
            pltpu.VMEM((PP * PP, WCH), BF16),
            pltpu.VMEM((WCH, PP * PP), F32),
            pltpu.VMEM((2, 80, BS), BF16),
            pltpu.VMEM((2, WCH * PP, WCH), BF16),
            pltpu.VMEM((WCH, PP * PP, PP * PP), BF16),
            pltpu.VMEM((GRP, PP, BS, BS), BF16),
            pltpu.VMEM((GRP, PP, BS, BS), BF16),
            pltpu.VMEM((2, PP, BS, BS), F32),
            pltpu.VMEM((16, BS), F32),
            pltpu.VMEM((NDEV, 16, BS), F32),
            dma,
            dma,
            dma,
            dma,
            dma((2,)),
            dma((2,)),
            dma((SEC, 2)),
            dma((SEC, 2)),
            dma((SEC, 2)),
            dma((SEC, 2)),
            dma,
            dma,
            dma,
            dma,
            dma((8,)),
            dma((2,)),
        ],
        compiler_params=pltpu.CompilerParams(
            collective_id=0, has_side_effects=True, vmem_limit_bytes=VMEM_LIMIT
        ),
        name="sweep",
    )(charges, lens, energy, labels, theta, tensors, mpo, benv, right, ops)


def on_device(
    theta,
    boundary_env,
    right_env,
    site_tensors,
    site_mpo,
    bond_ops,
    block_energy,
    sector_charge,
    block_len,
    channel_charge,
):
    mpo = jnp.transpose(site_mpo[0], (0, 1, 3, 4, 2)).reshape(2, WCH * PP, WCH)
    ops = jnp.transpose(bond_ops[0], (1, 2, 0)).reshape(PP * PP, WCH)
    lanczos, coef, env_out = sweep(
        channel_charge,
        block_len,
        block_energy,
        sector_charge,
        theta[0],
        site_tensors[0],
        mpo,
        boundary_env,
        right_env[0],
        ops,
    )
    return env_out[None], lanczos[None], coef


def solution(mesh):
    return jax.shard_map(
        on_device,
        mesh=mesh,
        in_specs=(
            P("site", ("blk", "charge"), None, None),
            P(("blk", "charge"), None, None, None),
            P("site", ("blk", "charge"), None, None, None),
            P("site", None, ("blk", "charge"), None, None, None),
            P("site", None, None, None, None, None),
            P("site", None, None, None),
            P("site", ("blk", "charge")),
            P("site", ("blk", "charge")),
            P("site", ("blk", "charge")),
            P(),
        ),
        out_specs=(
            P("site", ("blk", "charge"), None, None, None),
            P("site", ("blk", "charge"), None, None),
            P("site", None),
        ),
        check_vma=False,
    )
```

```python
import jax
import jax.numpy as jnp
from jax import lax
from jax.experimental import pallas as pl
from jax.experimental.pallas import tpu as pltpu
from jax.sharding import PartitionSpec as P

BS = 128
PH = 4
WCH = 18
WP = 24
MS = 73
CH = 128
GRP = 9
PRE = 0
PP = 16
M = 2048
NS = 64
SEC = 4
NBLK = 16
NDEV = 32
SIDE = 4
STEPS = (
    (1, 1), (3, 3), (2, 2), (1, 3), (3, 1), (2, 0), (0, 2), (1, 2),
    (3, 2), (2, 1), (2, 3), (1, 0), (3, 0), (0, 1), (0, 3),
)
F32 = jnp.float32
BF16 = jnp.bfloat16
MESH = pl.DeviceIdType.MESH
VMEM_LIMIT = 64 * 1024 * 1024 - 2400 * 1024


def mm(a, b):
    return jnp.dot(a, b, preferred_element_type=F32)


def loop(low, high, body):
    def step(i, carry):
        body(i)
        return carry

    lax.fori_loop(low, high, step, 0)


def env_site(a_ref, w_ref, l_ref, m_ref, at_ref, out_ref):
    for t in range(PH):
        at_ref[:, t * BS : (t + 1) * BS] = a_ref[t].T
    a_cat = jnp.concatenate([a_ref[s] for s in range(PH)], axis=1)
    w2 = w_ref[:, : PH * WP]

    def chunk(ci):
        base = pl.multiple_of(ci * (CH * WP), CH * WP)
        left = mm(l_ref[pl.ds(base, CH * WP), :].astype(BF16), a_cat)
        for j in range(0, CH, 2):
            sides = []
            for e in (j, j + 1):
                rows = left[e * WP : (e + 1) * WP]
                sides.append(
                    jnp.concatenate([rows[:, s * BS : (s + 1) * BS] for s in range(PH)], axis=0)
                )
            mixed = mm(w2, jnp.concatenate(sides, axis=1).astype(BF16))
            for e in range(2):
                m_ref[pl.ds((ci * CH + j + e) * MS, PH * WCH), :] = mixed[
                    : PH * WCH, e * BS : (e + 1) * BS
                ]

    loop(0, BS // CH, chunk)

    for v in range(0, WCH, 2):
        sides = []
        for e in range(2):
            sides.append(
                jnp.concatenate(
                    [m_ref[pl.ds(t * WCH + v + e, BS, stride=MS), :] for t in range(PH)], axis=0
                )
            )
        new = mm(at_ref[...], jnp.concatenate(sides, axis=1).astype(BF16))
        for e in range(2):
            one = new[:, e * BS : (e + 1) * BS]
            out_ref[v + e] = one.astype(BF16)
            l_ref[pl.ds(v + e, BS, stride=WP), :] = one


def iota(shape, dim):
    return lax.broadcasted_iota(jnp.int32, shape, dim)


def ones_where(condition):
    return jnp.where(condition, 1.0, 0.0).astype(BF16)


def first_dims(a, b):
    return lax.dot_general(a, b, (((0,), (0,)), ((), ())), preferred_element_type=F32)


def build_mixer(mpo_ref, mixer_ref):
    tall = (WCH * PP, BS)
    row, lane = iota(tall, 0), iota(tall, 1)
    wanted = lax.rem(row, PH) * WP + lax.div(row, PP)
    place = (80, WCH)
    for i in range(2):
        total = jnp.zeros((80, BS), F32)
        for t in range(PH):
            pick = ones_where((lax.rem(lax.div(row, PH), PH) == t) & (lane == wanted))
            part = first_dims(mpo_ref[i], pick).astype(BF16)
            put = ones_where(iota(place, 0) == t * WCH + iota(place, 1))
            total = total + mm(put, part)
        mixer_ref[i] = total.astype(BF16)


def build_kron(ops_ref, lines, kron):
    full = (PP * PP, PP * PP)
    row, lane = iota(full, 0), iota(full, 1)
    lines[...] = first_dims(ops_ref[...], ones_where(row == lane))
    spread = ones_where(lax.div(row, PP) == lax.div(lane, PP))

    def one(w):
        value = jnp.broadcast_to(lines[pl.ds(w, 1), :], full)
        here = jnp.where(lax.div(row, PP) == lax.rem(lane, PP), value, 0.0).astype(BF16)
        same = lax.rem(row, PP) == lax.rem(lane, PP)
        kron[w] = jnp.where(same, mm(here, spread), 0.0).astype(BF16)

    loop(0, WCH, one)


def block_product(charge_ref, kron, tiles, env_ref, right_ref, mixed, states, acc):
    def group(wi):
        for e in range(GRP):
            w = wi * GRP + e
            charge = charge_ref[w]
            c = jnp.where(charge == 0, 2, jnp.where(charge < 0, 0, 1))
            big = kron[w]
            for g in range(4):
                sides = []
                for h in range(2):
                    r0 = (g * 2 + h) * 16
                    sides.append(tiles[:, c, r0 : r0 + 16, :].reshape(PP * 16, BS))
                part = mm(big, jnp.concatenate(sides, axis=1)).astype(BF16)
                for h in range(2):
                    r0 = (g * 2 + h) * 16
                    mixed[e, :, r0 : r0 + 16, :] = part[:, h * BS : (h + 1) * BS].reshape(
                        PP, 16, BS
                    )
        for e in range(GRP):
            env = env_ref[wi * GRP + e]
            for t in range(0, PP, 2):
                part = mm(env, jnp.concatenate([mixed[e, t], mixed[e, t + 1]], axis=1))
                part = part.astype(BF16)
                states[e, t] = part[:, :BS]
                states[e, t + 1] = part[:, BS:]
        right = right_ref[pl.ds(wi * GRP, GRP)].reshape(GRP * BS, BS)
        for t in range(0, PP, 4):
            both = jnp.concatenate(
                [states[e, t : t + 4].reshape(4 * BS, BS) for e in range(GRP)], axis=1
            )
            acc[t : t + 4] += mm(both, right).reshape(4, BS, BS)

    acc[...] = jnp.zeros_like(acc)
    loop(0, WCH // GRP, group)


def sweep_kernel(
    charge_ref,
    len_ref,
    energy_ref,
    label_ref,
    theta_ref,
    tens_ref,
    mpo_ref,
    benv_ref,
    right_ref,
    ops_ref,
    lanczos_ref,
    coef_ref,
    envout_ref,
    tiles_a,
    tiles_b,
    recv1,
    send2,
    lab_mine,
    lab_all,
    table,
    table_s,
    tens,
    w2,
    left,
    mixer,
    at,
    envs,
    benv,
    right,
    ops,
    lines,
    w2_ref,
    mpo,
    kron,
    mixed,
    states,
    acc,
    mine,
    stats,
    lab_send,
    lab_recv,
    one_send,
    one_recv,
    two_send,
    two_recv,
    ten_send,
    ten_recv,
    w_send,
    w_recv,
    env_send,
    env_recv,
    stat_send,
    stat_recv,
    local,
    tile_sem,
):
    z = lax.axis_index("site")
    blk = lax.axis_index("blk")
    core = lax.axis_index("charge")
    me = blk * 2 + core
    first = lax.div(z, 3)
    other = 1 - first
    tiles = (tiles_a, tiles_b)
    order = (first, other)

    def ahead(dx, dy):
        return lax.rem(lax.div(blk, SIDE) + dx, SIDE) * SIDE + lax.rem(lax.rem(blk, SIDE) + dy, SIDE)

    def arrived(ref, sem):
        pltpu.make_async_copy(ref, ref, sem).wait()

    def plane(off):
        dev = lax.rem(me + off, NDEV)
        return {"blk": lax.div(dev, 2), "charge": lax.rem(dev, 2)}

    barrier = pltpu.get_barrier_semaphore()
    loop(
        1,
        NDEV,
        lambda off: pl.semaphore_signal(
            barrier, inc=1, device_id=plane(off), device_id_type=MESH
        ),
    )
    for off in range(1, SEC):
        pl.semaphore_signal(
            barrier, inc=1, device_id={"site": lax.rem(z + off, SEC)}, device_id_type=MESH
        )

    def tile_load(turn, s):
        return pltpu.make_async_copy(
            theta_ref.at[order[turn], :, pl.ds(pl.multiple_of(s * BS, BS), BS)],
            tiles[turn].at[s, 2],
            tile_sem.at[turn],
        )

    for turn in range(2):
        loop(0, PP, lambda s: tile_load(turn, s).start())
    loads = [
        pltpu.make_async_copy(benv_ref, benv, local.at[0]),
        pltpu.make_async_copy(tens_ref, tens.at[z], local.at[1]),
        pltpu.make_async_copy(right_ref, right, local.at[4]),
        pltpu.make_async_copy(ops_ref, ops, local.at[6]),
    ]
    load_mpo = pltpu.make_async_copy(mpo_ref, mpo, local.at[2])
    load_mpo.start()
    for copy in loads:
        copy.start()

    lane = lax.broadcasted_iota(jnp.int32, (8, BS), 1)
    line = lax.broadcasted_iota(jnp.int32, (8, BS), 0)
    row = jnp.zeros((8, BS), jnp.int32)
    for k in range(2):
        here = (line == core) & (lane == label_ref[0, k] + 1)
        row = row + jnp.where(here, 2 * blk + k + 1, 0)
        row = row + jnp.where((line == 2) & (lane == 2 * me + k), label_ref[0, k], 0)
    lab_mine[...] = row
    lab_all[me] = row
    recv1[0] = jnp.zeros((BS, BS), BF16)
    rows = lax.broadcasted_iota(jnp.int32, (BS, BS), 0)

    def mask(s):
        for turn in range(2):
            tile = tiles[turn][s, 2].astype(F32)
            tiles[turn][s, 2] = jnp.where(rows < len_ref[0, order[turn]], tile, 0.0).astype(BF16)

    for turn in range(2):
        arrived(tiles[turn].at[:, 2], tile_sem.at[turn])
    loop(0, PP, mask)
    load_mpo.wait()
    build_mixer(mpo, w2_ref)
    for k in range(2):
        w2[z, k] = w2_ref[...]
    for turn in range(2):
        recv1[1 + 2 * blk + order[turn]] = tiles[turn][blk, 2]
    pl.semaphore_wait(barrier, NDEV - 1 + SEC - 1)

    def labels_to(off):
        return pltpu.make_async_remote_copy(
            src_ref=lab_mine,
            dst_ref=lab_all.at[me],
            send_sem=lab_send,
            recv_sem=lab_recv,
            device_id=plane(off),
            device_id_type=MESH,
        )

    def piece_to(turn, dev):
        return pltpu.make_async_remote_copy(
            src_ref=tiles[turn].at[dev, 2],
            dst_ref=recv1.at[1 + 2 * blk + order[turn]],
            send_sem=one_send,
            recv_sem=one_recv,
            device_id={"blk": dev},
            device_id_type=MESH,
        )

    def picked_to(turn, dev):
        return pltpu.make_async_remote_copy(
            src_ref=send2.at[turn, dev],
            dst_ref=tiles[turn].at[blk, pl.ds(0, 2)],
            send_sem=two_send.at[turn],
            recv_sem=two_recv.at[turn],
            device_id={"blk": dev, "charge": 1 - core},
            device_id_type=MESH,
        )

    def tensors_to(dst, k, sec):
        return pltpu.make_async_remote_copy(
            src_ref=tens_ref.at[:, k],
            dst_ref=tens.at[z, :, k],
            send_sem=ten_send.at[dst, k],
            recv_sem=ten_recv.at[sec, k],
            device_id={"site": dst},
            device_id_type=MESH,
        )

    def mixer_to(dst, k, sec):
        return pltpu.make_async_remote_copy(
            src_ref=w2_ref,
            dst_ref=w2.at[z, k],
            send_sem=w_send.at[dst, k],
            recv_sem=w_recv.at[sec, k],
            device_id={"site": dst},
            device_id_type=MESH,
        )

    routes = (
        (0, 3, 1), (0, 2, 0), (0, 1, 0), (0, 1, 1),
        (1, 3, 1), (1, 2, 0), (2, 3, 1),
    )

    loop(1, NDEV, lambda off: labels_to(off).start())
    for src, dst, k in routes:

        @pl.when(z == src)
        def _():
            mixer_to(dst, k, src).start()
            tensors_to(dst, k, src).start()

    for turn in range(2):
        for dx, dy in STEPS:
            piece_to(turn, ahead(dx, dy)).start()

    for copy in loads:
        copy.wait()
    build_kron(ops, lines, kron)

    def load_left(k, env_ref):
        left[k] = jnp.zeros((BS * WP, BS), F32)

        def one(v):
            left[k, pl.ds(v, BS, stride=WP), :] = env_ref[v].astype(F32)

        loop(0, WCH, one)

    for k in range(2):

        @pl.when((z < 2) | (z == k + 2))
        def _():
            load_left(k, benv.at[k])

        @pl.when(z == 0)
        def _():
            envs[0, k] = benv[k]

    def send_picked():
        arrived(lab_all.at[pl.ds(0, NDEV - 1)], lab_recv)
        total = jnp.zeros((8, BS), jnp.int32)
        for i in range(NDEV):
            total = total + lab_all[i]
        table[...] = total
        to_scalar = pltpu.make_async_copy(table, table_s, local.at[5])
        to_scalar.start()
        to_scalar.wait()
        arrived(recv1.at[pl.ds(0, 2 * NBLK - 2)], one_recv)
        for turn in range(2):

            def pick(dev):
                label = table_s[2, 4 * dev + 2 * (1 - core) + order[turn]]
                for gi in range(2):
                    send2[turn, dev, gi] = recv1[table_s[core, label + 2 * gi]]

            loop(0, NBLK, pick)
            for dx, dy in STEPS + ((0, 0),):
                picked_to(turn, ahead(dx, dy)).start()

    def env_to(slot, k, dst):
        return pltpu.make_async_remote_copy(
            src_ref=envs.at[slot, k],
            dst_ref=envs.at[0, k],
            send_sem=env_send,
            recv_sem=env_recv,
            device_id={"site": dst},
            device_id_type=MESH,
        )

    env_routes = ((2, 5, 1, 0, 3), (3, 3, 2, 1, 2))

    def site(q):
        unit, i = lax.div(q, 2), lax.rem(q, 2)
        sec = jnp.where(z < 2, lax.div(unit, 2), unit)
        k = jnp.where(z < 2, lax.rem(unit, 2), z - 2)

        @pl.when(q == PRE)
        def _():
            send_picked()

        @pl.when((i == 0) & (sec != z))
        def _():
            mixer_to(0, k, sec).wait_recv()
            tensors_to(0, k, sec).wait_recv()

        slot = jnp.where(sec == z, 1, 0)
        slot = jnp.where((z == 3) & (sec == 1), 2, slot)
        env_site(tens.at[sec, i, k], w2.at[sec, k, i], left.at[k], mixer, at, envs.at[slot, k])
        for src, when, slot_at, kk, dst in env_routes:

            @pl.when((z == src) & (q == when))
            def _():
                env_to(slot_at, kk, dst).start()

    loop(0, jnp.where(z == 0, 4, jnp.where(z == 2, 6, 8)), site)

    def late_sites():
        env_to(0, 0, 0).wait_recv()
        load_left(other, envs.at[0, other])

        def late(i):
            env_site(
                tens.at[z, i, other], w2.at[z, other, i], left.at[other], mixer, at, envs.at[1, other]
            )

        loop(0, 2, late)

    zero = jnp.zeros((8, BS), F32)

    def fold(x):
        return jnp.sum(x.reshape(16, 8, BS), axis=0)

    def everywhere(x):
        return jnp.broadcast_to(
            jnp.sum(jnp.sum(x, axis=0, keepdims=True), axis=1, keepdims=True), (1, BS)
        )

    def block_sums(turn):
        length, energy = len_ref[0, order[turn]], energy_ref[0, order[turn]]

        def sums_one(t, carry):
            cor, nor = carry
            th = tiles[turn][t, 2].astype(F32)
            p = jnp.where(rows < length, acc[turn, t], 0.0) - energy * th
            acc[turn, t] = p
            return cor + fold(p * th), nor + fold(th * th)

        cor, nor = lax.fori_loop(0, PP, sums_one, (zero, zero))
        cor, nor = everywhere(cor), everywhere(nor)
        rho = jnp.where(nor > 0, cor / jnp.where(nor > 0, nor, 1.0), 0.0)

        def sums_two(t, carry):
            sq, cross = carry
            th = tiles[turn][t, 2].astype(F32)
            r = acc[turn, t] - rho * th
            return sq + fold(r * r), cross + fold(r * th)

        sq, cross = lax.fori_loop(0, PP, sums_two, (zero, zero))
        mine[8 * turn : 8 * turn + 8] = jnp.concatenate(
            [cor, nor, everywhere(sq), everywhere(cross), rho, jnp.zeros((3, BS), F32)], axis=0
        )

    for turn in range(2):
        k = order[turn]
        if turn:
            pl.when(z >= 2)(late_sites)
            env_store = pltpu.make_async_copy(envs.at[1], envout_ref, local.at[7])
            env_store.start()
        arrived(tiles[turn].at[:, pl.ds(0, 2)], two_recv.at[turn])
        block_product(
            charge_ref, kron, tiles[turn], envs.at[0, k], right.at[k], mixed, states, acc.at[turn]
        )
        block_sums(turn)


    stats[me] = mine[...]

    def stat_to(off):
        return pltpu.make_async_remote_copy(
            src_ref=mine,
            dst_ref=stats.at[me],
            send_sem=stat_send,
            recv_sem=stat_recv,
            device_id=plane(off),
            device_id_type=MESH,
        )

    loop(1, NDEV, lambda off: stat_to(off).start())
    arrived(lab_all.at[pl.ds(0, NDEV - 1)], lab_send)
    arrived(recv1.at[pl.ds(0, 2 * NBLK - 2)], one_send)
    for turn in range(2):
        arrived(send2.at[turn], two_send.at[turn])
    for src, dst, k in routes:

        @pl.when(z == src)
        def _():
            mixer_to(dst, k, src).wait_send()
            tensors_to(dst, k, src).wait_send()

    for src, when, slot_at, kk, dst in env_routes:

        @pl.when(z == src)
        def _():
            env_to(slot_at, kk, dst).wait_send()

    arrived(stats.at[pl.ds(0, NDEV - 1)], stat_recv)

    cor_all = jnp.zeros((1, BS), F32)
    nor_all = jnp.zeros((1, BS), F32)
    for i in range(NDEV):
        for at_row in (0, 8):
            cor_all = cor_all + stats[i, at_row : at_row + 1]
            nor_all = nor_all + stats[i, at_row + 1 : at_row + 2]
    ray = cor_all / nor_all
    res = jnp.zeros((1, BS), F32)
    for i in range(NDEV):
        for at_row in (0, 8):
            nor, sq, cross, rho = (
                stats[i, at_row + j : at_row + j + 1] for j in (1, 2, 3, 4)
            )
            gap = rho - ray
            res = res + (sq + gap * (2.0 * cross + gap * nor))
    mean_sq = jnp.maximum(res, 0.0) / (NS * BS * M)
    scale = 1.0 / jnp.sqrt(mean_sq + 1e-06)

    def finish(t):
        for turn in range(2):
            th = tiles[turn][t, 2].astype(F32)
            lanczos_ref[order[turn], :, pl.ds(pl.multiple_of(t * BS, BS), BS)] = (
                (acc[turn, t] - ray * th) * scale
            ).astype(BF16)

    loop(0, PP, finish)
    coef_ref[0, 0] = ray[0, 0]
    coef_ref[0, 1] = jnp.sqrt(mean_sq)[0, 0]
    arrived(stats.at[pl.ds(0, NDEV - 1)], stat_send)
    env_store.wait()


def sweep(charges, lens, energy, labels, theta, tensors, mpo, benv, right, ops):
    hbm = pl.BlockSpec(memory_space=pltpu.HBM)
    vmem = pl.BlockSpec(memory_space=pltpu.VMEM)
    smem = pl.BlockSpec(memory_space=pltpu.SMEM)
    dma = pltpu.SemaphoreType.DMA
    return pl.pallas_call(
        sweep_kernel,
        out_shape=(
            pltpu.VMEM((2, BS, M), BF16),
            jax.ShapeDtypeStruct((1, 2), F32),
            pltpu.VMEM((2, WCH, BS, BS), BF16),
        ),
        in_specs=[smem] * 4 + [hbm] * 6,
        out_specs=(vmem, smem, vmem),
        scratch_shapes=[
            pltpu.VMEM((PP, 3, BS, BS), BF16),
            pltpu.VMEM((PP, 3, BS, BS), BF16),
            pltpu.VMEM((NDEV + 1, BS, BS), BF16),
            pltpu.VMEM((2, NBLK, 2, BS, BS), BF16),
            pltpu.VMEM((8, BS), jnp.int32),
            pltpu.VMEM((NDEV, 8, BS), jnp.int32),
            pltpu.VMEM((8, BS), jnp.int32),
            pltpu.SMEM((8, BS), jnp.int32),
            pltpu.VMEM((SEC, 2, 2, PH, BS, BS), BF16),
            pltpu.VMEM((SEC, 2, 2, 80, BS), BF16),
            pltpu.VMEM((2, BS * WP, BS), F32),
            pltpu.VMEM((BS * MS, BS), F32),
            pltpu.VMEM((BS, PH * BS), BF16),
            pltpu.VMEM((3, 2, WCH, BS, BS), BF16),
            pltpu.VMEM((2, WCH, BS, BS), BF16),
            pltpu.VMEM((2, WCH, BS, BS), BF16),
            pltpu.VMEM((PP * PP, WCH), BF16),
            pltpu.VMEM((WCH, PP * PP), F32),
            pltpu.VMEM((2, 80, BS), BF16),
            pltpu.VMEM((2, WCH * PP, WCH), BF16),
            pltpu.VMEM((WCH, PP * PP, PP * PP), BF16),
            pltpu.VMEM((GRP, PP, BS, BS), BF16),
            pltpu.VMEM((GRP, PP, BS, BS), BF16),
            pltpu.VMEM((2, PP, BS, BS), F32),
            pltpu.VMEM((16, BS), F32),
            pltpu.VMEM((NDEV, 16, BS), F32),
            dma,
            dma,
            dma,
            dma,
            dma((2,)),
            dma((2,)),
            dma((SEC, 2)),
            dma((SEC, 2)),
            dma((SEC, 2)),
            dma((SEC, 2)),
            dma,
            dma,
            dma,
            dma,
            dma((8,)),
            dma((2,)),
        ],
        compiler_params=pltpu.CompilerParams(
            collective_id=0, has_side_effects=True, vmem_limit_bytes=VMEM_LIMIT
        ),
        name="sweep",
    )(charges, lens, energy, labels, theta, tensors, mpo, benv, right, ops)


def on_device(
    theta,
    boundary_env,
    right_env,
    site_tensors,
    site_mpo,
    bond_ops,
    block_energy,
    sector_charge,
    block_len,
    channel_charge,
):
    mpo = jnp.transpose(site_mpo[0], (0, 1, 3, 4, 2)).reshape(2, WCH * PP, WCH)
    ops = jnp.transpose(bond_ops[0], (1, 2, 0)).reshape(PP * PP, WCH)
    lanczos, coef, env_out = sweep(
        channel_charge,
        block_len,
        block_energy,
        sector_charge,
        theta[0],
        site_tensors[0],
        mpo,
        boundary_env,
        right_env[0],
        ops,
    )
    return env_out[None], lanczos[None], coef


def solution(mesh):
    return jax.shard_map(
        on_device,
        mesh=mesh,
        in_specs=(
            P("site", ("blk", "charge"), None, None),
            P(("blk", "charge"), None, None, None),
            P("site", ("blk", "charge"), None, None, None),
            P("site", None, ("blk", "charge"), None, None, None),
            P("site", None, None, None, None, None),
            P("site", None, None, None),
            P("site", ("blk", "charge")),
            P("site", ("blk", "charge")),
            P("site", ("blk", "charge")),
            P(),
        ),
        out_specs=(
            P("site", ("blk", "charge"), None, None, None),
            P("site", ("blk", "charge"), None, None),
            P("site", None),
        ),
        check_vma=False,
    )
```
